32 devices in a mesh: tm: 8 (over y, x, core), mp: 4 (over z).
Axes of the slice: x: 2, y: 2, z: 4, core: 2. Of those that a mesh axis runs over, the one named last changes fastest.
Arguments:
- frames: bfloat16 [4096, 1024], P(('tm', 'mp')), may hold values from -6 to 6
- block_ids: int32 [4096], replicated, may hold values from 0 to 203, never falling along the last dimension, each value on 1 to 40 neighbouring positions
- valid_counts: int32 [8], replicated, may hold values from 1 to 512, as said below
- norm_attn: float32 [1024], replicated, may hold values from 0.25 to 1.75
- w_qkv: bfloat16 [1024, 3072], replicated, may hold values from -1 to 1
- w_attn_out: bfloat16 [1024, 1024], replicated, may hold values from -0.1875 to 0.1875
- norm_conv: float32 [1024], replicated, may hold values from 0.25 to 1.75
- w_point_in: bfloat16 [1024, 2048], replicated, may hold values from -0.1875 to 0.1875
- w_depth: bfloat16 [31, 1024], replicated, may hold values from -1 to 1
- w_point_out: bfloat16 [1024, 1024], replicated, may hold values from -0.1875 to 0.1875
- w_adapter: bfloat16 [1024, 8192], P('tm', 'mp'), may hold values from -1 to 1
- llm_gain: float32 [8192], replicated, may hold values from 0.25 to 1.75
- w_query: bfloat16 [8192, 8192], P('tm', 'mp'), may hold values from -1 to 1
- w_key: bfloat16 [8192, 1024], P('tm', 'mp'), may hold values from -1 to 1
- w_value: bfloat16 [8192, 1024], P('tm', 'mp'), may hold values from -0.0625 to 0.0625
Outputs:
- conf_out: bfloat16 [4096, 1024], P(('tm', 'mp'))
- attended: bfloat16 [1024, 8192], P('tm', 'mp')
The draws below stay inside these ranges and needn't reach their ends.
Inputs may be any that keep to these rules, and one draw needn't show every extreme that they name: `block_ids`: block numbers never fall along the recording, and one block holds 1 to 40 frames. Every time shard but the last holds 512 real frames; the frames after the first valid_counts[t] of time shard t are padding.
All inputs are finite; a program needn't handle non-finite values.
Results may differ from the reference program's by a relative error of at most 0.014.
Values may be sent and summed in bfloat16 or wider, within the bound.
No kernel may reach another device: no remote copies, remote signals or barrier semaphores. Data moves between devices by JAX's collectives and lax.ppermute only.
A program may use at most 192 MiB of HBM per device.

```python
import math
import jax
import jax.numpy as jnp
import numpy as np
from jax import lax

CD = 1024
CH = 16
CHD = 64
KER = 31
SPAN = 40
FR = 128
HD = 8192
QH = 64
KVH = 8
HDIM = 128
SHARDS = 8
SHARD_FR = 512
FRAMES = 4096
TS = 128
TOKENS = 1024


def drawn_normal(key, salt, shape, scale):
    values = jax.random.normal(jax.random.fold_in(key, salt), shape, jnp.float32)
    return jnp.clip(values, -6.0, 6.0) * scale


def draw_valid_counts(key, part):
    last_count = jax.random.randint(jax.random.fold_in(key, 21), (1,), 1, SHARD_FR + 1).astype(jnp.int32)
    full_counts = jnp.full((SHARDS - 1,), SHARD_FR, jnp.int32)
    return jnp.concatenate([full_counts, last_count], axis=0)


def draw_frames(key, part):
    return drawn_normal(key, 1, (FRAMES, CD), 1.0).astype(jnp.bfloat16)


def draw_w_qkv(key, part):
    scale = CD ** (-0.5)
    return drawn_normal(key, 2, (CD, 3 * CD), scale).astype(jnp.bfloat16)


def draw_w_adapter(key, part):
    scale = CD ** (-0.5)
    return drawn_normal(key, 3, (CD, HD), scale).astype(jnp.bfloat16)


def draw_w_query(key, part):
    scale = HD ** (-0.5)
    return drawn_normal(key, 4, (HD, QH * HDIM), scale).astype(jnp.bfloat16)


def draw_w_key(key, part):
    scale = HD ** (-0.5)
    return drawn_normal(key, 5, (HD, KVH * HDIM), scale).astype(jnp.bfloat16)


def steps_of(stream_key, shape, split, low, high):
    factor_of, own = 1.0, jax.random.fold_in(stream_key, 6)
    for dim, shards_of in split:
        heights = jnp.exp(jax.random.uniform(jax.random.fold_in(own, dim), (shards_of,), jnp.float32, low / len(split), high / len(split)))
        factor_of = factor_of * jnp.repeat(heights, shape[dim] // shards_of).reshape([-1 if axis == dim else 1 for axis in range(len(shape))])
    return factor_of


def split_up(count, total, bound, slope):
    weights = [(1 << 20) // math.isqrt(rank ** slope) + 1 for rank in range(2, count + 1)]
    spare, given = total - bound - (count - 1), [1] * (count - 1)
    while spare > 0:
        candidates = [i for i in range(count - 1) if given[i] < bound]
        pool, left = sum([weights[i] for i in candidates]), spare
        for i in candidates:
            extra = min(bound - given[i], max(1, left * weights[i] // pool), spare)
            given[i] = given[i] + extra
            spare = spare - extra
    return np.array([bound] + given)


def ragged_sizes(rng, count, total, most, slope):
    if count == 2:
        one = jax.random.randint(rng, (), max(1, total - most), min(most, total - 1) + 1)
        return jnp.stack([one, total - one])
    sizes = jnp.asarray(split_up(count, total, most, slope), jnp.int32)
    pairs = (count - 1) // 2
    source_of, taker = sizes[1:1 + 2 * pairs:2], sizes[2:2 + 2 * pairs:2]
    room = jnp.minimum(source_of - 1, most - taker)
    passed = jax.random.randint(jax.random.fold_in(rng, 1), (pairs,), 0, 1 << 20) % (room + 1)
    sizes = sizes.at[1:1 + 2 * pairs:2].set(source_of - passed).at[2:2 + 2 * pairs:2].set(taker + passed)
    return sizes[jax.random.permutation(jax.random.fold_in(rng, 2), count)]


def centred(rng, extent, scale, limit, split=(), kind=jnp.bfloat16):
    loudness = steps_of(rng, extent, split, -0.22, 0.18) if split else 1.0
    array = jax.random.normal(rng, extent, jnp.float32) * scale * loudness
    return jnp.minimum(jnp.maximum(array, -limit), limit).astype(kind)


def setup_inputs(seed: int = 0) -> dict:
    splits = jax.random.split(jax.random.key(seed), 16)
    frames = draw_frames(jax.random.fold_in(splits[15], 71), 0)
    block_ids = jnp.searchsorted(jnp.cumsum(ragged_sizes(splits[1], FRAMES * 2 // SPAN, FRAMES, SPAN, 1)), jnp.arange(FRAMES), side="right").astype(jnp.int32)
    valid_counts = draw_valid_counts(jax.random.fold_in(splits[15], 71), 0)
    norm_attn = jnp.clip(1.0 + 0.15 * jax.random.normal(splits[3], (CD,), jnp.float32), 0.25, 1.75)
    w_qkv = draw_w_qkv(jax.random.fold_in(splits[15], 71), 0)
    w_attn_out = centred(splits[5], (CD, CD), CD ** -0.5, 0.1875)
    norm_conv = jnp.clip(1.0 + 0.15 * jax.random.normal(splits[6], (CD,), jnp.float32), 0.25, 1.75)
    w_point_in = centred(splits[7], (CD, 2 * CD), CD ** -0.5, 0.1875)
    w_depth = centred(splits[8], (KER, CD), KER ** -0.5, 1.0)
    w_point_out = centred(splits[9], (CD, CD), CD ** -0.5, 0.1875)
    w_adapter = draw_w_adapter(jax.random.fold_in(splits[15], 71), 0)
    llm_gain = jnp.clip(1.0 + 0.15 * jax.random.normal(splits[11], (HD,), jnp.float32), 0.25, 1.75)
    w_query = draw_w_query(jax.random.fold_in(splits[15], 71), 0)
    w_key = draw_w_key(jax.random.fold_in(splits[15], 71), 0)
    w_value = centred(splits[14], (HD, KVH * HDIM), HD ** -0.5, 0.0625, ((0, 8), (1, 4)))
    return {"frames": frames, "block_ids": block_ids, "valid_counts": valid_counts, "norm_attn": norm_attn, "w_qkv": w_qkv, "w_attn_out": w_attn_out, "norm_conv": norm_conv, "w_point_in": w_point_in, "w_depth": w_depth, "w_point_out": w_point_out, "w_adapter": w_adapter, "llm_gain": llm_gain, "w_query": w_query, "w_key": w_key, "w_value": w_value}


eps_conf = 1e-05
eps_llm = 1e-06
rope_base = 1000000.0
masked_score = -1e+30

def shard_count(index, valid_counts, shard_len):
    shard = index // shard_len
    table = jnp.arange(valid_counts.shape[0], dtype=jnp.int32)
    hit = shard[:, None] == table[None, :]
    count = lax.optimization_barrier(jnp.sum(jnp.where(hit, valid_counts[None, :], 0), axis=1))
    return (index - shard * shard_len, count)

def layer_norm(field, gain):
    center = field - lax.optimization_barrier(jnp.mean(field, axis=-1, keepdims=True))
    spread = lax.optimization_barrier(jnp.mean(center * center, axis=-1, keepdims=True))
    return center * lax.rsqrt(spread + eps_conf) * gain

def rotary(field, positions):
    half = field.shape[-1] // 2
    freq = rope_base ** (-(jnp.arange(half, dtype=jnp.float32) * 2.0) / field.shape[-1])
    angle = positions.astype(jnp.float32)[:, None] * freq[None, :]
    cosine = jnp.concatenate([jnp.cos(angle), jnp.cos(angle)], axis=-1)[:, None, :]
    sine = jnp.concatenate([jnp.sin(angle), jnp.sin(angle)], axis=-1)[:, None, :]
    turned = jnp.concatenate([-field[..., half:], field[..., :half]], axis=-1)
    return field * cosine + turned * sine

def reference(frames, block_ids, valid_counts, norm_attn, w_qkv, w_attn_out, norm_conv, w_point_in, w_depth, w_point_out, w_adapter, llm_gain, w_query, w_key, w_value):
    inputs = frames.astype(jnp.float32)
    frame_index = jnp.arange(FRAMES, dtype=jnp.int32)
    place, count = shard_count(frame_index, valid_counts, SHARD_FR)
    frame_real = place < count
    normed = layer_norm(inputs, norm_attn).astype(jnp.bfloat16)
    projected = jnp.dot(normed, w_qkv, preferred_element_type=jnp.float32).astype(jnp.bfloat16)
    queries = projected[:, :CD]
    pad_keys = jnp.concatenate([jnp.zeros((FR, CD), jnp.bfloat16), projected[:, CD:2 * CD]], axis=0)
    pad_values = jnp.concatenate([jnp.zeros((FR, CD), jnp.bfloat16), projected[:, 2 * CD:]], axis=0)
    pad_blocks = jnp.concatenate([jnp.full((FR,), -100, jnp.int32), block_ids], axis=0)
    pad_real = jnp.concatenate([jnp.zeros((FR,), bool), frame_real], axis=0)

    def one_block(block):
        begin = block * FR
        query = lax.dynamic_slice_in_dim(queries, begin, FR, 0).astype(jnp.float32).reshape(FR, CH, CHD)
        keys = lax.dynamic_slice_in_dim(pad_keys, begin, 2 * FR, 0).astype(jnp.float32).reshape(2 * FR, CH, CHD)
        values = lax.dynamic_slice_in_dim(pad_values, begin, 2 * FR, 0).astype(jnp.float32).reshape(2 * FR, CH, CHD)
        key_block_id = lax.dynamic_slice_in_dim(pad_blocks, begin, 2 * FR, 0)
        key_real = lax.dynamic_slice_in_dim(pad_real, begin, 2 * FR, 0)
        query_block_id = lax.dynamic_slice_in_dim(block_ids, begin, FR, 0)
        query_index = begin + jnp.arange(FR, dtype=jnp.int32)
        key_index = begin - FR + jnp.arange(2 * FR, dtype=jnp.int32)
        same = key_index[None, :] == query_index[:, None]
        visible = (key_index[None, :] <= query_index[:, None]) & (key_block_id[None, :] >= query_block_id[:, None] - 2) & (key_real[None, :] | same)
        scores = jnp.einsum('qhd,khd->hqk', query, keys) / jnp.sqrt(jnp.float32(CHD))
        scores = jnp.where(visible[None], scores, masked_score)
        top = lax.optimization_barrier(jnp.max(scores, axis=-1, keepdims=True))
        weights = jnp.where(visible[None], jnp.exp(scores - top), 0.0)
        total = lax.optimization_barrier(jnp.sum(weights, axis=-1))
        rounded = lax.optimization_barrier(weights.astype(jnp.bfloat16)).astype(jnp.float32)
        summed = jnp.einsum('hqk,khd->hqd', rounded, values)
        context = summed / total[..., None]
        return jnp.transpose(context, (1, 0, 2)).reshape(FR, CD).astype(jnp.bfloat16)
    conf_context = lax.map(one_block, jnp.arange(FRAMES // FR, dtype=jnp.int32)).reshape(FRAMES, CD)
    mid = inputs + jnp.dot(conf_context, w_attn_out, preferred_element_type=jnp.float32)
    conv_in = layer_norm(mid, norm_conv).astype(jnp.bfloat16)
    both = jnp.dot(conv_in, w_point_in, preferred_element_type=jnp.float32)
    glu = both[:, :CD] * jax.nn.sigmoid(both[:, CD:])
    glu = jnp.where(frame_real[:, None], glu, 0.0).astype(jnp.bfloat16)
    padded = jnp.concatenate([jnp.zeros((KER - 1, CD), jnp.float32), glu.astype(jnp.float32)], axis=0)
    kernel = w_depth.astype(jnp.float32)
    depth = jnp.zeros((FRAMES, CD), jnp.float32)
    for tap in range(KER):
        depth = depth + kernel[tap][None, :] * padded[KER - 1 - tap:KER - 1 - tap + FRAMES]
    activated = jax.nn.silu(depth).astype(jnp.bfloat16)
    final = mid + jnp.dot(activated, w_point_out, preferred_element_type=jnp.float32)
    conf_out = jnp.where(frame_real[:, None], final, 0.0).astype(jnp.bfloat16)
    pooled = (lax.optimization_barrier(jnp.sum(conf_out.astype(jnp.float32).reshape(TOKENS, 4, CD), axis=1)) * 0.25).astype(jnp.bfloat16)
    adapted = jnp.dot(pooled, w_adapter, preferred_element_type=jnp.float32)
    llm_in = (adapted * lax.rsqrt(lax.optimization_barrier(jnp.mean(adapted * adapted, axis=-1, keepdims=True)) + eps_llm) * llm_gain).astype(jnp.bfloat16)
    token_index = jnp.arange(TOKENS, dtype=jnp.int32)
    token_place, token_count = shard_count(token_index, valid_counts, TS)
    token_real = token_place * 4 < token_count
    group = QH // KVH
    raw_query = jnp.dot(llm_in, w_query, preferred_element_type=jnp.float32).reshape(TOKENS, QH, HDIM)
    raw_keys = jnp.dot(llm_in, w_key, preferred_element_type=jnp.float32).reshape(TOKENS, KVH, HDIM)
    llm_query = rotary(raw_query, token_index).astype(jnp.bfloat16)
    llm_keys = rotary(raw_keys, token_index).astype(jnp.bfloat16)
    llm_values = jnp.dot(llm_in, w_value, preferred_element_type=jnp.float32).astype(jnp.bfloat16).reshape(TOKENS, KVH, HDIM)
    block_rows = min(512, TOKENS)
    query_blocks = llm_query.reshape(TOKENS // block_rows, block_rows, KVH, group, HDIM)

    def query_block(index):
        query = query_blocks[index]
        query_index = index * block_rows + jnp.arange(block_rows, dtype=jnp.int32)
        same = token_index[None, :] == query_index[:, None]
        visible = (token_index[None, :] <= query_index[:, None]) & (token_real[None, :] | same)

        def one_head(head):
            head_query = lax.dynamic_index_in_dim(query, head, 1, keepdims=False).astype(jnp.float32)
            head_keys = lax.dynamic_index_in_dim(llm_keys, head, 1, keepdims=False).astype(jnp.float32)
            head_values = lax.dynamic_index_in_dim(llm_values, head, 1, keepdims=False).astype(jnp.float32)
            scores = jnp.einsum('qgd,kd->gqk', head_query, head_keys) / jnp.sqrt(jnp.float32(HDIM))
            scores = jnp.where(visible[None], scores, masked_score)
            top = lax.optimization_barrier(jnp.max(scores, axis=-1, keepdims=True))
            weights = jnp.where(visible[None], jnp.exp(scores - top), 0.0)
            total = lax.optimization_barrier(jnp.sum(weights, axis=-1))
            rounded = lax.optimization_barrier(weights.astype(jnp.bfloat16)).astype(jnp.float32)
            return jnp.einsum('gqk,kd->gqd', rounded, head_values) / total[..., None]
        heads_out = lax.map(one_head, jnp.arange(KVH, dtype=jnp.int32))
        return jnp.transpose(heads_out, (2, 0, 1, 3)).reshape(block_rows, QH * HDIM).astype(jnp.bfloat16)
    attended = lax.map(query_block, jnp.arange(TOKENS // block_rows, dtype=jnp.int32)).reshape(TOKENS, QH * HDIM)
    return (conf_out, attended)
```

```python
import jax
import jax.numpy as jnp
from jax import lax
from jax.experimental import pallas as pl
from jax.experimental.pallas import tpu as pltpu
from jax.sharding import PartitionSpec as P

CH = 16
HDIM = 128
SPAN = 40


eps_conf = 1e-05
eps_llm = 1e-06
rope_base = 1000000.0
masked_score = -1e30


def shifted(value, axis, by):
    length = lax.axis_size(axis)
    return lax.ppermute(value, axis, [(i, i + by) for i in range(length - by)])


def swapped(value, bits):
    length = lax.axis_size("tm")
    return lax.ppermute(value, "tm", [(i, i ^ bits) for i in range(length)])


def rotated(value, by):
    length = lax.axis_size("mp")
    return lax.ppermute(value, "mp", [(i, (i + by) % length) for i in range(length)])


def shard_count(index, valid_counts, shard_len):
    shard = index // shard_len
    table = jnp.arange(valid_counts.shape[0], dtype=jnp.int32)
    hit = shard[:, None] == table[None, :]
    count = jnp.sum(jnp.where(hit, valid_counts[None, :], 0), axis=1)
    return (index - shard * shard_len, count)


def layer_norm(field, gain):
    center = field - jnp.mean(field, axis=-1, keepdims=True)
    spread = jnp.mean(center * center, axis=-1, keepdims=True)
    return center * lax.rsqrt(spread + eps_conf) * gain


def rotary_tables(positions, size):
    half = size // 2
    freq = rope_base ** (-(jnp.arange(half, dtype=jnp.float32) * 2.0) / size)
    angle = positions.astype(jnp.float32)[:, None] * freq[None, :]
    cosine = jnp.concatenate([jnp.cos(angle), jnp.cos(angle)], axis=-1)
    sine = jnp.concatenate([-jnp.sin(angle), jnp.sin(angle)], axis=-1)
    return cosine, sine


def turn(field, cosine, sine):
    return field * cosine + pltpu.roll(field, HDIM // 2, 1) * sine


def total_of(refs, columns):
    parts = [ref[:, columns].astype(jnp.float32) for ref in refs]
    while len(parts) > 1:
        parts = [sum(parts[i : i + 2]) for i in range(0, len(parts), 2)]
    return parts[0]


def finish_keys(parts, cosine, sine, key_cols, width):
    rows = cosine.shape[0]

    def kernel(*refs):
        part_refs, (cos_ref, sin_ref, kv_ref, scale_ref) = refs[: len(parts)], refs[len(parts) :]
        squares = total_of(part_refs, pl.ds(2 * key_cols, HDIM))
        power = (
            squares[:, 0:1] + squares[:, 32:33] + squares[:, 64:65] + squares[:, 96:97]
        ) * (1.0 / width)
        scale = lax.rsqrt(power + eps_llm)
        scale_ref[...] = jnp.broadcast_to(scale, scale_ref.shape)
        for head in range(key_cols // HDIM):
            columns = pl.ds(head * HDIM, HDIM)
            raw = total_of(part_refs, columns) * scale
            kv_ref[:, columns] = turn(raw, cos_ref[...], sin_ref[...]).astype(jnp.bfloat16)
        columns = pl.ds(key_cols, key_cols)
        kv_ref[:, columns] = (total_of(part_refs, columns) * scale).astype(jnp.bfloat16)

    return pl.pallas_call(
        kernel,
        out_shape=(
            jax.ShapeDtypeStruct((rows, 2 * key_cols), jnp.bfloat16),
            jax.ShapeDtypeStruct((rows, HDIM), jnp.float32),
        ),
        name="finish_keys",
    )(*parts, cosine, sine)


def attend(parts, kv, scale, cosine, sine, query_place, key_place, key_real, kv_heads):
    rows, query_cols = parts[0].shape
    tokens = kv.shape[0]
    group = query_cols // HDIM // kv_heads
    step = 2 if group % 2 == 0 and tokens <= 2048 else 1
    factor = HDIM**-0.5

    def kernel(*refs):
        part_refs = refs[: len(parts)]
        scale_ref, cos_ref, sin_ref, at_ref, place_ref, real_ref, key_ref, value_ref, out_ref = refs[
            len(parts) :
        ]
        at, place = at_ref[...], place_ref[...]
        seen = (place <= at) & ((real_ref[...] > 0) | (place == at))
        bias = jnp.where(seen, 0.0, masked_score)
        bias = jnp.concatenate([bias] * step, axis=0)
        keys, values = key_ref[...], value_ref[...]
        for first in range(0, group, step):
            queries = []
            for head in range(first, first + step):
                raw = total_of(part_refs, pl.ds(head * HDIM, HDIM)) * scale_ref[...]
                queries.append(turn(raw, cos_ref[...], sin_ref[...]).astype(jnp.bfloat16))
            query = jnp.concatenate(queries, axis=0)
            scores = lax.dot_general(
                query, keys, (((1,), (1,)), ((), ())), preferred_element_type=jnp.float32
            )
            scores = scores * factor + bias
            top = jnp.max(scores, axis=-1, keepdims=True)
            weights = jnp.exp(scores - top)
            total = jnp.sum(weights, axis=-1, keepdims=True)
            summed = jnp.dot(
                weights.astype(jnp.bfloat16), values, preferred_element_type=jnp.float32
            )
            result = (summed / total).astype(jnp.bfloat16)
            for i in range(step):
                out_ref[:, pl.ds((first + i) * HDIM, HDIM)] = result[i * rows : (i + 1) * rows]

    whole = lambda shape: pl.BlockSpec(shape, lambda h: (0, 0))
    return pl.pallas_call(
        kernel,
        grid=(kv_heads,),
        in_specs=[pl.BlockSpec((rows, group * HDIM), lambda h: (0, h))] * len(parts)
        + [
            whole((rows, HDIM)),
            whole((rows, HDIM)),
            whole((rows, HDIM)),
            whole((rows, 1)),
            whole((1, tokens)),
            whole((1, tokens)),
            pl.BlockSpec((tokens, HDIM), lambda h: (0, h)),
            pl.BlockSpec((tokens, HDIM), lambda h: (0, kv_heads + h)),
        ],
        out_specs=pl.BlockSpec((rows, group * HDIM), lambda h: (0, h)),
        out_shape=jax.ShapeDtypeStruct((rows, query_cols), jnp.bfloat16),
        compiler_params=pltpu.CompilerParams(vmem_limit_bytes=48 << 20),
        name="attend",
    )(*parts, scale, cosine, sine, query_place, key_place, key_real, kv, kv)


def conformer(
    frames, near, far, first, block_ids, valid_counts, shard_frames, norm_attn, w_qkv, w_attn_out,
    norm_conv, w_point_in, w_depth, w_point_out,
):
    frame_rows, width = frames.shape
    heads, head_size = CH, width // CH
    extra = far.shape[0]
    before = near.shape[0] + extra
    held = jnp.concatenate([far, near, frames], axis=0).astype(jnp.float32)
    key_rows, query_rows = before + frame_rows, extra + frame_rows
    lead = key_rows - query_rows
    normed = layer_norm(held, norm_attn).astype(jnp.bfloat16)
    projected = jnp.dot(normed, w_qkv, preferred_element_type=jnp.float32).astype(jnp.bfloat16)
    queries = projected[lead:, :width].reshape(query_rows, heads, head_size)
    keys = projected[:, width : 2 * width].reshape(key_rows, heads, head_size)
    values = projected[:, 2 * width :].reshape(key_rows, heads, head_size)
    key_index = first - before + jnp.arange(key_rows, dtype=jnp.int32)
    key_place, key_count = shard_count(key_index, valid_counts, shard_frames)
    key_real = (key_place < key_count) & (key_index >= 0)
    padded_ids = jnp.concatenate([jnp.full((before,), -100, jnp.int32), block_ids])
    key_ids = lax.dynamic_slice_in_dim(padded_ids, first, key_rows, 0)
    query_index, query_ids, real = key_index[lead:], key_ids[lead:], key_real[lead:]
    same = key_index[None, :] == query_index[:, None]
    visible = (
        (key_index[None, :] <= query_index[:, None])
        & (key_ids[None, :] >= query_ids[:, None] - 2)
        & (key_real[None, :] | same)
    )
    scores = jnp.einsum("qhd,khd->hqk", queries, keys, preferred_element_type=jnp.float32) / jnp.sqrt(
        jnp.float32(head_size)
    )
    scores = jnp.where(visible[None], scores, masked_score)
    top = jnp.max(scores, axis=-1, keepdims=True)
    weights = jnp.where(visible[None], jnp.exp(scores - top), 0.0)
    total = jnp.sum(weights, axis=-1)
    summed = jnp.einsum(
        "hqk,khd->qhd", weights.astype(jnp.bfloat16), values, preferred_element_type=jnp.float32
    )
    context = (
        (summed / jnp.transpose(total)[:, :, None]).reshape(query_rows, width).astype(jnp.bfloat16)
    )
    mid = held[lead:] + jnp.dot(context, w_attn_out, preferred_element_type=jnp.float32)
    conv_in = layer_norm(mid, norm_conv).astype(jnp.bfloat16)
    both = jnp.dot(conv_in, w_point_in, preferred_element_type=jnp.float32)
    glu = both[:, :width] * jax.nn.sigmoid(both[:, width:])
    glu = jnp.where(real[:, None], glu, 0.0).astype(jnp.bfloat16).astype(jnp.float32)
    taps = w_depth.shape[0]
    kernel = w_depth.astype(jnp.float32)
    depth = jnp.zeros((frame_rows, width), jnp.float32)
    for tap in range(taps):
        depth = depth + kernel[tap][None, :] * glu[extra - tap : extra - tap + frame_rows]
    activated = jax.nn.silu(depth).astype(jnp.bfloat16)
    final = mid[extra:] + jnp.dot(activated, w_point_out, preferred_element_type=jnp.float32)
    conf_out = jnp.where(real[extra:, None], final, 0.0).astype(jnp.bfloat16)
    pooled = (
        jnp.sum(conf_out.astype(jnp.float32).reshape(frame_rows // 4, 4, width), axis=1) * 0.25
    ).astype(jnp.bfloat16)
    return conf_out, pooled


def own_adapter_columns(w_adapter):
    tm_count, mp_count = lax.axis_size("tm"), lax.axis_size("mp")
    time_place, model_place = lax.axis_index("tm"), lax.axis_index("mp")
    rows, cols = w_adapter.shape
    pieces = [w_adapter] + [rotated(w_adapter, by) for by in range(1, mp_count)]
    stacked = jnp.stack(pieces)
    kept = {}
    for other in range(0, tm_count, 2):
        wanted = (time_place ^ other) // 2
        piece = lax.dynamic_index_in_dim(
            stacked, (model_place - wanted) % mp_count, 0, keepdims=False
        )
        kept[other] = swapped(piece, other) if other else piece
    near = jnp.stack([kept[other] for other in range(0, tm_count, 2)])
    half = cols // 2
    core = time_place % 2
    mine = lax.dynamic_slice_in_dim(near, core * half, half, 2)
    given = lax.dynamic_slice_in_dim(near, (1 - core) * half, half, 2)
    taken = swapped(given, 1)
    result = jnp.zeros((tm_count, rows, half), w_adapter.dtype)
    for i in range(tm_count // 2):
        result = lax.dynamic_update_index_in_dim(result, mine[i], time_place ^ (2 * i), 0)
        result = lax.dynamic_update_index_in_dim(result, taken[i], time_place ^ (2 * i + 1), 0)
    return result.reshape(tm_count * rows, half)


def spread(value):
    tm_count = lax.axis_size("tm")
    blocks = [value] + [swapped(value, other) for other in range(2, tm_count, 2)]
    even = jnp.concatenate(blocks, axis=0)
    return jnp.concatenate([even, swapped(even, 1)], axis=0)


def gathered_parts(value):
    tm_count = lax.axis_size("tm")
    half = value.shape[0] // 2
    rows = value.shape[0] // tm_count
    other = swapped(value[half:], 1)
    chip = (value[:half].astype(jnp.float32) + other.astype(jnp.float32)).astype(jnp.bfloat16)
    return [chip[:rows]] + [
        swapped(chip[i * rows : (i + 1) * rows], 2 * i) for i in range(1, tm_count // 2)
    ]


def on_device(
    frames,
    block_ids,
    valid_counts,
    norm_attn,
    w_qkv,
    w_attn_out,
    norm_conv,
    w_point_in,
    w_depth,
    w_point_out,
    w_adapter,
    llm_gain,
    w_query,
    w_key,
    w_value,
):
    tm_count, mp_count = lax.axis_size("tm"), lax.axis_size("mp")
    time_place, model_place = lax.axis_index("tm"), lax.axis_index("mp")
    frame_rows, width = frames.shape
    shard_frames = frame_rows * mp_count
    first = (time_place * mp_count + model_place) * frame_rows
    near = shifted(frames, ("tm", "mp"), 1)
    far = shifted(frames[frame_rows - 32 :], ("tm", "mp"), 2)
    adapter = own_adapter_columns(w_adapter)
    conf_out, pooled = conformer(
        frames, near, far, first, block_ids, valid_counts, shard_frames, norm_attn, w_qkv,
        w_attn_out, norm_conv, w_point_in, w_depth, w_point_out,
    )
    piece = pooled.shape[0]
    shard_tokens = piece * mp_count
    cycle = [rotated(pooled, by) for by in range(mp_count - 1, 0, -1)] + [pooled]
    shard_pooled = lax.dynamic_slice_in_dim(
        jnp.concatenate(cycle + cycle, axis=0), (mp_count - 1 - model_place) * piece, shard_tokens, 0
    )
    all_pooled = spread(shard_pooled)
    tokens = all_pooled.shape[0]
    adapted = jnp.dot(all_pooled, adapter, preferred_element_type=jnp.float32)
    block = adapter.shape[1]
    gain = lax.dynamic_slice_in_dim(llm_gain, time_place * block, block, 0)
    scaled = (adapted * gain).astype(jnp.bfloat16)
    squares = jnp.sum(adapted * adapted, axis=-1, keepdims=True)
    high = lax.reduce_precision(squares, 8, 7)
    lane = jnp.arange(HDIM, dtype=jnp.int32)[None, :] // 32 - 2 * (time_place % 2)
    words = jnp.where(lane == 0, high, jnp.where(lane == 1, squares - high, 0.0)).astype(jnp.bfloat16)
    raw_keys = jnp.dot(scaled, w_key, preferred_element_type=jnp.float32).astype(jnp.bfloat16)
    raw_values = jnp.dot(scaled, w_value, preferred_element_type=jnp.float32).astype(jnp.bfloat16)
    raw_query = jnp.dot(scaled, w_query, preferred_element_type=jnp.float32).astype(jnp.bfloat16)
    key_cols = w_key.shape[1]
    kv_parts = gathered_parts(jnp.concatenate([raw_keys, raw_values, words], axis=1))
    query_parts = gathered_parts(raw_query)
    order = list(range(0, tm_count, 2)) + list(range(1, tm_count, 2))
    within = jnp.arange(shard_tokens, dtype=jnp.int32)
    own_place = time_place * shard_tokens + within
    cosine, sine = rotary_tables(own_place, HDIM)
    kv, scale = finish_keys(kv_parts, cosine, sine, key_cols, block * tm_count)
    all_kv = spread(kv)
    key_place = jnp.concatenate([(time_place ^ other) * shard_tokens + within for other in order])
    place_in, counts = shard_count(key_place, valid_counts, shard_tokens)
    key_real = (place_in * 4 < counts).astype(jnp.int32)
    attended = attend(
        query_parts, all_kv, scale, cosine, sine, own_place[:, None], key_place[None, :],
        key_real[None, :], key_cols // HDIM,
    )
    return (conf_out, attended)


def solution(mesh):
    placed = (
        P(("tm", "mp"), None),
        P(),
        P(),
        P(),
        P(),
        P(),
        P(),
        P(),
        P(),
        P(),
        P("tm", "mp"),
        P(),
        P("tm", "mp"),
        P("tm", "mp"),
        P("tm", "mp"),
    )
    return jax.shard_map(
        on_device,
        mesh=mesh,
        in_specs=placed,
        out_specs=(P(("tm", "mp"), None), P("tm", "mp")),
        check_vma=False,
    )
```

```python
import jax
import jax.numpy as jnp
from jax import lax
from jax.experimental import pallas as pl
from jax.experimental.pallas import tpu as pltpu
from jax.sharding import PartitionSpec as P

CH = 16
HDIM = 128
SPAN = 40


eps_conf = 1e-05
eps_llm = 1e-06
rope_base = 1000000.0
masked_score = -1e30


def shifted(value, axis, by):
    length = lax.axis_size(axis)
    return lax.ppermute(value, axis, [(i, i + by) for i in range(length - by)])


def swapped(value, bits):
    length = lax.axis_size("tm")
    return lax.ppermute(value, "tm", [(i, i ^ bits) for i in range(length)])


def rotated(value, by):
    length = lax.axis_size("mp")
    return lax.ppermute(value, "mp", [(i, (i + by) % length) for i in range(length)])


def shard_count(index, valid_counts, shard_len):
    shard = index // shard_len
    table = jnp.arange(valid_counts.shape[0], dtype=jnp.int32)
    hit = shard[:, None] == table[None, :]
    count = jnp.sum(jnp.where(hit, valid_counts[None, :], 0), axis=1)
    return (index - shard * shard_len, count)


def layer_norm(field, gain):
    center = field - jnp.mean(field, axis=-1, keepdims=True)
    spread = jnp.mean(center * center, axis=-1, keepdims=True)
    return center * lax.rsqrt(spread + eps_conf) * gain


def rotary_tables(positions, size):
    half = size // 2
    freq = rope_base ** (-(jnp.arange(half, dtype=jnp.float32) * 2.0) / size)
    angle = positions.astype(jnp.float32)[:, None] * freq[None, :]
    cosine = jnp.concatenate([jnp.cos(angle), jnp.cos(angle)], axis=-1)
    sine = jnp.concatenate([-jnp.sin(angle), jnp.sin(angle)], axis=-1)
    return cosine, sine


def turn(field, cosine, sine):
    return field * cosine + pltpu.roll(field, HDIM // 2, 1) * sine


def total_of(refs, columns):
    parts = [ref[:, columns].astype(jnp.float32) for ref in refs]
    while len(parts) > 1:
        parts = [sum(parts[i : i + 2]) for i in range(0, len(parts), 2)]
    return parts[0]


def finish_keys(parts, cosine, sine, key_cols, width):
    rows = cosine.shape[0]

    def kernel(*refs):
        part_refs, (cos_ref, sin_ref, kv_ref, scale_ref) = refs[: len(parts)], refs[len(parts) :]
        squares = total_of(part_refs, pl.ds(2 * key_cols, HDIM))
        power = (
            squares[:, 0:1] + squares[:, 32:33] + squares[:, 64:65] + squares[:, 96:97]
        ) * (1.0 / width)
        scale = lax.rsqrt(power + eps_llm)
        scale_ref[...] = jnp.broadcast_to(scale, scale_ref.shape)
        for head in range(key_cols // HDIM):
            columns = pl.ds(head * HDIM, HDIM)
            raw = total_of(part_refs, columns) * scale
            kv_ref[:, columns] = turn(raw, cos_ref[...], sin_ref[...]).astype(jnp.bfloat16)
        columns = pl.ds(key_cols, key_cols)
        kv_ref[:, columns] = (total_of(part_refs, columns) * scale).astype(jnp.bfloat16)

    return pl.pallas_call(
        kernel,
        out_shape=(
            jax.ShapeDtypeStruct((rows, 2 * key_cols), jnp.bfloat16),
            jax.ShapeDtypeStruct((rows, HDIM), jnp.float32),
        ),
        name="finish_keys",
    )(*parts, cosine, sine)


def attend(chunks, kv, scale, cosine, sine, query_place, key_place, key_real, kv_heads):
    count, each = len(chunks), len(chunks[0])
    rows, chunk_cols = chunks[0][0].shape
    tokens = kv.shape[0]
    chunk_heads = chunk_cols // HDIM
    group = count * chunk_heads // kv_heads
    step = 2 if chunk_heads % 2 == 0 and tokens <= 2048 else 1
    factor = HDIM**-0.5

    def kernel(*refs):
        part_refs = refs[: count * each]
        scale_ref, cos_ref, sin_ref, at_ref, place_ref, real_ref, kv_ref, out_ref = refs[count * each :]
        at, place = at_ref[...], place_ref[...]
        seen = (place <= at) & ((real_ref[...] > 0) | (place == at))
        bias = jnp.where(seen, 0.0, masked_score)
        bias = jnp.concatenate([bias] * step, axis=0)
        for first in range(0, count * chunk_heads, step):
            refs_here = part_refs[first // chunk_heads * each : (first // chunk_heads + 1) * each]
            kv_head = first // group
            queries = []
            for head in range(first % chunk_heads, first % chunk_heads + step):
                raw = total_of(refs_here, pl.ds(head * HDIM, HDIM)) * scale_ref[...]
                queries.append(turn(raw, cos_ref[...], sin_ref[...]).astype(jnp.bfloat16))
            scores = lax.dot_general(
                jnp.concatenate(queries, axis=0),
                kv_ref[:, pl.ds(kv_head * HDIM, HDIM)],
                (((1,), (1,)), ((), ())),
                preferred_element_type=jnp.float32,
            )
            scores = scores * factor + bias
            top = jnp.max(scores, axis=-1, keepdims=True)
            weights = jnp.exp(scores - top)
            total = jnp.sum(weights, axis=-1, keepdims=True)
            summed = jnp.dot(
                weights.astype(jnp.bfloat16),
                kv_ref[:, pl.ds((kv_heads + kv_head) * HDIM, HDIM)],
                preferred_element_type=jnp.float32,
            )
            result = (summed / total).astype(jnp.bfloat16)
            for i in range(step):
                out_ref[:, pl.ds((first + i) * HDIM, HDIM)] = result[i * rows : (i + 1) * rows]

    flat = [part for chunk in chunks for part in chunk]
    return pl.pallas_call(
        kernel,
        out_shape=jax.ShapeDtypeStruct((rows, count * chunk_cols), jnp.bfloat16),
        compiler_params=pltpu.CompilerParams(vmem_limit_bytes=40 << 20),
        name="attend",
    )(*flat, scale, cosine, sine, query_place, key_place, key_real, kv)


def project(held, gain, w_qkv):
    rows, width = held.shape
    wide = w_qkv.shape[1]
    step = width

    def kernel(held_ref, gain_ref, weight_ref, out_ref, normed_ref):
        @pl.when(pl.program_id(0) == 0)
        def _():
            normed_ref[...] = layer_norm(held_ref[...].astype(jnp.float32), gain_ref[...]).astype(
                jnp.bfloat16
            )

        out_ref[...] = jnp.dot(
            normed_ref[...], weight_ref[...], preferred_element_type=jnp.float32
        ).astype(jnp.bfloat16)

    return pl.pallas_call(
        kernel,
        grid=(wide // step,),
        in_specs=[
            pl.BlockSpec((rows, width), lambda i: (0, 0)),
            pl.BlockSpec((1, width), lambda i: (0, 0)),
            pl.BlockSpec((width, step), lambda i: (0, i)),
        ],
        out_specs=pl.BlockSpec((rows, step), lambda i: (0, i)),
        out_shape=jax.ShapeDtypeStruct((rows, wide), jnp.bfloat16),
        scratch_shapes=[pltpu.VMEM((rows, width), jnp.bfloat16)],
        compiler_params=pltpu.CompilerParams(vmem_limit_bytes=16 << 20),
        cost_estimate=pl.CostEstimate(
            flops=2 * rows * width * wide, bytes_accessed=2 * width * wide, transcendentals=0
        ),
        name="project",
    )(held, gain[None, :], w_qkv)


def convolve(
    frames, near, own_proj, before_proj, key_index, key_ids, key_real, w_attn_out, norm_conv,
    w_point_in, w_depth, w_point_out,
):
    frame_rows, width = frames.shape
    before = before_proj.shape[0]
    key_rows = before + frame_rows
    near_rows = near.shape[0]
    extra = before - near_rows
    query_rows = extra + frame_rows
    lead = key_rows - query_rows
    head_size = width // CH
    pooled_rows = frame_rows // 4
    taps = w_depth.shape[0]
    lanes = 2 * head_size

    def kernel(
        frames_ref, near_ref, own_ref, before_ref, key_row_ref, query_col_ref, gain_ref, depth_ref,
        attn_hbm, in_hbm, out_hbm, conf_ref, pooled_ref,
        attn_w, in_w, out_w, context_ref, glu_ref, active_ref, sems,
    ):
        copies = [
            pltpu.make_async_copy(source, target, sems.at[i])
            for i, (source, target) in enumerate(
                ((attn_hbm, attn_w), (in_hbm, in_w), (out_hbm, out_w))
            )
        ]
        for copy in copies:
            copy.start()
        key_at, key_id, key_live = key_row_ref[0:1], key_row_ref[1:2], key_row_ref[2:3]
        at, ids, live = query_col_ref[:, 0:1], query_col_ref[:, 1:2], query_col_ref[:, 2:3]
        seen = (key_at <= at) & (key_id >= ids - 2) & ((key_live > 0) | (key_at == at))
        bias = jnp.where(seen, 0.0, masked_score)
        bias = jnp.concatenate([bias, bias], axis=0)
        left = lax.broadcasted_iota(jnp.int32, (query_rows, lanes), 1) < head_size
        for pair in range(width // lanes):

            def both_rows(offset):
                columns = pl.ds(offset + pair * lanes, lanes)
                return jnp.concatenate([before_ref[:, columns], own_ref[:, columns]], axis=0)

            query = both_rows(0)[lead:]
            none = jnp.zeros_like(query)
            query = jnp.concatenate(
                [jnp.where(left, query, none), jnp.where(left, none, query)], axis=0
            )
            scores = lax.dot_general(
                query, both_rows(width), (((1,), (1,)), ((), ())), preferred_element_type=jnp.float32
            )
            scores = scores * head_size**-0.5 + bias
            top = jnp.max(scores, axis=-1, keepdims=True)
            weights = jnp.exp(scores - top)
            total = jnp.sum(weights, axis=-1, keepdims=True)
            summed = jnp.dot(
                weights.astype(jnp.bfloat16), both_rows(2 * width), preferred_element_type=jnp.float32
            )
            context = summed / total
            context_ref[:, pl.ds(pair * lanes, lanes)] = jnp.where(
                left, context[:query_rows], context[query_rows:]
            ).astype(jnp.bfloat16)
        inputs = jnp.concatenate([near_ref[near_rows - extra :], frames_ref[...]], axis=0)
        copies[0].wait()
        mid = inputs.astype(jnp.float32) + jnp.dot(
            context_ref[...], attn_w[...], preferred_element_type=jnp.float32
        )
        conv_in = layer_norm(mid, gain_ref[...]).astype(jnp.bfloat16)
        copies[1].wait()
        part = 256
        for start in range(0, width, part):
            value = jnp.dot(
                conv_in, in_w[:, pl.ds(start, part)], preferred_element_type=jnp.float32
            )
            gate = jnp.dot(
                conv_in, in_w[:, pl.ds(width + start, part)], preferred_element_type=jnp.float32
            )
            glu = jnp.where(live > 0, value * jax.nn.sigmoid(gate), 0.0)
            glu_ref[:, pl.ds(start, part)] = glu.astype(jnp.bfloat16).astype(jnp.float32)
        for start in range(0, width, 128):
            columns = pl.ds(start, 128)
            depth = jnp.zeros((frame_rows, 128), jnp.float32)
            for tap in range(taps):
                depth = depth + depth_ref[tap : tap + 1, columns] * glu_ref[
                    pl.ds(extra - tap, frame_rows), columns
                ]
            active_ref[:, columns] = jax.nn.silu(depth).astype(jnp.bfloat16)
        copies[2].wait()
        final = mid[extra:] + jnp.dot(
            active_ref[...], out_w[...], preferred_element_type=jnp.float32
        )
        conf = jnp.where(live[extra:] > 0, final, 0.0).astype(jnp.bfloat16)
        conf_ref[...] = conf
        row = lax.broadcasted_iota(jnp.int32, (pooled_rows, frame_rows), 0)
        column = lax.broadcasted_iota(jnp.int32, (pooled_rows, frame_rows), 1)
        mean = jnp.where(column // 4 == row, 0.25, 0.0).astype(jnp.bfloat16)
        pooled_ref[...] = jnp.dot(mean, conf, preferred_element_type=jnp.float32).astype(
            jnp.bfloat16
        )

    key_row = jnp.stack([key_index, key_ids, key_real.astype(jnp.int32)])
    query_col = jnp.transpose(key_row[:, lead:])
    plain = pl.BlockSpec(memory_space=pltpu.VMEM)
    apart = pl.BlockSpec(memory_space=pl.ANY)
    flops = 2 * query_rows * width * 4 * width
    return pl.pallas_call(
        kernel,
        in_specs=[plain] * 8 + [apart] * 3,
        out_specs=(plain, plain),
        out_shape=(
            jax.ShapeDtypeStruct((frame_rows, width), jnp.bfloat16),
            jax.ShapeDtypeStruct((pooled_rows, width), jnp.bfloat16),
        ),
        scratch_shapes=[
            pltpu.VMEM(w_attn_out.shape, jnp.bfloat16),
            pltpu.VMEM(w_point_in.shape, jnp.bfloat16),
            pltpu.VMEM(w_point_out.shape, jnp.bfloat16),
            pltpu.VMEM((query_rows, width), jnp.bfloat16),
            pltpu.VMEM((query_rows, width), jnp.float32),
            pltpu.VMEM((frame_rows, width), jnp.bfloat16),
            pltpu.SemaphoreType.DMA((3,)),
        ],
        compiler_params=pltpu.CompilerParams(vmem_limit_bytes=32 << 20),
        cost_estimate=pl.CostEstimate(
            flops=flops, bytes_accessed=8 * width * width, transcendentals=CH * query_rows * key_rows
        ),
        name="convolve",
    )(
        frames, near, own_proj, before_proj, key_row, query_col, norm_conv[None, :],
        w_depth.astype(jnp.float32), w_attn_out, w_point_in, w_point_out,
    )


def conformer(
    frames, own_proj, near, far, first, block_ids, valid_counts, shard_frames, norm_attn, w_qkv,
    w_attn_out, norm_conv, w_point_in, w_depth, w_point_out,
):
    frame_rows = frames.shape[0]
    before = near.shape[0] + far.shape[0]
    key_rows = before + frame_rows
    before_proj = project(jnp.concatenate([far, near], axis=0), norm_attn, w_qkv)
    key_index = first - before + jnp.arange(key_rows, dtype=jnp.int32)
    key_place, key_count = shard_count(key_index, valid_counts, shard_frames)
    key_real = (key_place < key_count) & (key_index >= 0)
    padded_ids = jnp.concatenate([jnp.full((before,), -100, jnp.int32), block_ids])
    key_ids = lax.dynamic_slice_in_dim(padded_ids, first, key_rows, 0)
    return convolve(
        frames, near, own_proj, before_proj, key_index, key_ids, key_real, w_attn_out, norm_conv,
        w_point_in, w_depth, w_point_out,
    )


def line_pieces(value, beside):
    mp_count, place = lax.axis_size("mp"), lax.axis_index("mp")
    if mp_count != 4:
        pieces = [value] + [rotated(value, by) for by in range(1, mp_count)]
        return [jnp.stack(pieces)], lambda source: (place - source) % mp_count, beside
    below = lax.ppermute(value, "mp", [(0, 1), (1, 2), (2, 3)])
    above = lax.ppermute(value, "mp", [(1, 0), (2, 1), (3, 2)])
    value, below, above, beside = lax.optimization_barrier((value, below, above, beside))
    half = value.shape[0] // 2
    chunks, waiting = [], (value, below, above)
    for start in (0, half):
        mine, lower, upper = [array[start : start + half] for array in waiting]
        far = lax.ppermute(mine, "mp", [(0, 3), (3, 0)])
        lower_2 = lax.ppermute(lower, "mp", [(1, 2), (2, 3)])
        upper_2 = lax.ppermute(upper, "mp", [(2, 1), (1, 0)])
        if start == 0:
            far, lower_2, upper_2, waiting = lax.optimization_barrier(
                (far, lower_2, upper_2, waiting)
            )
        chunks.append(jnp.stack([far, lower_2, lower, mine, upper, upper_2]))
    return chunks, lambda source: (source - place + 3) % 6, beside


def chip_adapter_columns(stacked, row_of):
    tm_count = lax.axis_size("tm")
    time_place = lax.axis_index("tm")
    kept = []
    for other in range(0, tm_count, 2):
        wanted = (time_place ^ other) // 2
        piece = lax.dynamic_index_in_dim(stacked, row_of(wanted), 0, keepdims=False)
        kept.append(swapped(piece, other) if other else piece)
    return kept


def adapt(pooled, near, gain):
    tm_count, time_place = lax.axis_size("tm"), lax.axis_index("tm")
    part, cols = near[0][0].shape
    half = cols // 2
    tokens, depth = pooled.shape
    flat = [array for chunk in near for array in chunk]
    place_word = time_place.reshape(1).astype(jnp.int32)
    plain = pl.BlockSpec(memory_space=pltpu.VMEM)
    scalar = pl.BlockSpec(memory_space=pltpu.SMEM)

    def other_half(place_ref, *refs):
        columns = pl.ds(pl.multiple_of((1 - place_ref[0] % 2) * half, 128), half)
        for i, ref in enumerate(refs[:-1]):
            refs[-1][i * part : (i + 1) * part, :] = ref[:, columns]

    given = pl.pallas_call(
        other_half,
        in_specs=[scalar] + [plain] * len(flat),
        out_specs=plain,
        out_shape=jax.ShapeDtypeStruct((len(flat) * part, half), jnp.bfloat16),
        compiler_params=pltpu.CompilerParams(vmem_limit_bytes=16 << 20),
        name="other_half",
    )(place_word, *flat)
    taken = swapped(given, 1)
    step = min(256, tokens)

    def kernel(place_ref, *refs):
        near_refs = refs[: len(flat)]
        taken_ref, pooled_ref, gain_ref, out_ref, word_ref, weight_ref = refs[len(flat) :]
        place = place_ref[0]
        columns = pl.ds(pl.multiple_of((place % 2) * half, 128), half)
        for i, ref in enumerate(near_refs):
            chunk, other = i // (tm_count // 2), 2 * (i % (tm_count // 2))
            for shift in (0, 1):
                source = place ^ (other + shift)
                row = pl.multiple_of(source * (part * len(near)) + chunk * part, part)
                if shift:
                    weight_ref[pl.ds(row, part), :] = taken_ref[i * part : (i + 1) * part]
                else:
                    weight_ref[pl.ds(row, part), :] = ref[:, columns]
        lane = lax.broadcasted_iota(jnp.int32, (step, HDIM), 1) // 32 - 2 * (place % 2)
        for start in range(0, tokens, step):
            rows = pl.ds(start, step)
            adapted = jnp.dot(
                pooled_ref[rows, :], weight_ref[...], preferred_element_type=jnp.float32
            )
            out_ref[rows, :] = (adapted * gain_ref[...]).astype(jnp.bfloat16)
            squares = jnp.sum(adapted * adapted, axis=-1, keepdims=True)
            high = squares.astype(jnp.bfloat16).astype(jnp.float32)
            words = jnp.where(lane == 0, high, jnp.where(lane == 1, squares - high, 0.0))
            word_ref[rows, :] = words.astype(jnp.bfloat16)

    return pl.pallas_call(
        kernel,
        in_specs=[scalar] + [plain] * (len(flat) + 3),
        out_specs=(plain, plain),
        out_shape=(
            jax.ShapeDtypeStruct((tokens, half), jnp.bfloat16),
            jax.ShapeDtypeStruct((tokens, HDIM), jnp.bfloat16),
        ),
        scratch_shapes=[pltpu.VMEM((depth, half), jnp.bfloat16)],
        compiler_params=pltpu.CompilerParams(vmem_limit_bytes=48 << 20),
        name="adapt",
    )(place_word, *flat, taken, pooled, gain[None, :])


def spread_even(value):
    tm_count = lax.axis_size("tm")
    blocks = [value] + [swapped(value, other) for other in range(2, tm_count, 2)]
    return jnp.concatenate(blocks, axis=0)


def spread(even):
    return jnp.concatenate([even, swapped(even, 1)], axis=0)


def both_sum(one, other):
    return (one.astype(jnp.float32) + other.astype(jnp.float32)).astype(jnp.bfloat16)


def direct_parts(value):
    tm_count = lax.axis_size("tm")
    half = value.shape[0] // 2
    rows = value.shape[0] // tm_count
    chip = both_sum(value[:half], swapped(value[half:], 1))
    return [chip[:rows]] + [
        swapped(chip[i * rows : (i + 1) * rows], 2 * i) for i in range(1, tm_count // 2)
    ]


def chip_sum(left, right, weight):
    def product(rows):
        return jnp.dot(rows, weight, preferred_element_type=jnp.float32)

    other = swapped(product(right).astype(jnp.bfloat16), 1)
    return (product(left) + other.astype(jnp.float32)).astype(jnp.bfloat16)


def halved(held, bit, axes):
    axis = axes.index(bit)
    keep = lax.index_in_dim(held, 0, axis, keepdims=False)
    given = lax.index_in_dim(held, 1, axis, keepdims=False)
    return keep, swapped(given, 2 << bit), axes[:axis] + axes[axis + 1 :]


def on_device(
    frames,
    block_ids,
    valid_counts,
    norm_attn,
    w_qkv,
    w_attn_out,
    norm_conv,
    w_point_in,
    w_depth,
    w_point_out,
    w_adapter,
    llm_gain,
    w_query,
    w_key,
    w_value,
):
    tm_count, mp_count = lax.axis_size("tm"), lax.axis_size("mp")
    time_place, model_place = lax.axis_index("tm"), lax.axis_index("mp")
    frame_rows, width = frames.shape
    shard_frames = frame_rows * mp_count
    first = (time_place * mp_count + model_place) * frame_rows
    near = shifted(frames, ("tm", "mp"), 1)
    far = shifted(frames[frame_rows - 32 :], ("tm", "mp"), 2)
    own_proj = project(frames, norm_attn, w_qkv)
    stacked, row_of, (near, far, own_proj) = line_pieces(w_adapter, (near, far, own_proj))
    conf_out, pooled = conformer(
        frames, own_proj, near, far, first, block_ids, valid_counts, shard_frames, norm_attn, w_qkv,
        w_attn_out, norm_conv, w_point_in, w_depth, w_point_out,
    )
    pooled, stacked[0] = lax.optimization_barrier((pooled, stacked[0]))
    piece = pooled.shape[0]
    shard_tokens = piece * mp_count
    cycle = [rotated(pooled, by) for by in range(mp_count - 1, 0, -1)] + [pooled]
    shard_pooled = lax.dynamic_slice_in_dim(
        jnp.concatenate(cycle + cycle, axis=0), (mp_count - 1 - model_place) * piece, shard_tokens, 0
    )
    all_pooled, near_columns = lax.optimization_barrier(
        (
            spread(spread_even(shard_pooled)),
            [chip_adapter_columns(chunk, row_of) for chunk in stacked],
        )
    )
    tokens = all_pooled.shape[0]
    block = w_adapter.shape[1] * mp_count // tm_count
    gain = lax.dynamic_slice_in_dim(llm_gain, time_place * block, block, 0)
    scaled, words = adapt(all_pooled, near_columns, gain)
    raw_keys = jnp.dot(scaled, w_key, preferred_element_type=jnp.float32).astype(jnp.bfloat16)
    raw_values = jnp.dot(scaled, w_value, preferred_element_type=jnp.float32).astype(jnp.bfloat16)
    key_cols, half_cols = w_key.shape[1], w_query.shape[1] // 2
    kv_raw, scaled = lax.optimization_barrier(
        (jnp.concatenate([raw_keys, raw_values, words], axis=1), scaled)
    )
    kv_parts = direct_parts(kv_raw)
    bits = list(range(tm_count.bit_length() - 2))
    left, right = scaled[: tokens // 2], scaled[tokens // 2 :]
    sums = [
        chip_sum(left, right, w_query[:, :half_cols]),
        chip_sum(left, right, w_query[:, half_cols:]),
    ]
    kv_parts, _ = lax.optimization_barrier((kv_parts, sums))
    query_chunks, rest = [], [bits, bits[::-1]]
    for held, turns in zip(sums, rest):
        held = held.reshape((2,) * len(bits) + (shard_tokens, half_cols))
        keep, taken, left_axes = halved(held, turns[0], bits[::-1])
        for turn_bit in turns[1:]:
            keep, taken, left_axes = halved(both_sum(keep, taken), turn_bit, left_axes)
        query_chunks.append((keep, taken))
    order = list(range(0, tm_count, 2)) + list(range(1, tm_count, 2))
    within = jnp.arange(shard_tokens, dtype=jnp.int32)
    own_place = time_place * shard_tokens + within
    cosine, sine = rotary_tables(own_place, HDIM)
    kv, scale = finish_keys(kv_parts, cosine, sine, key_cols, block * tm_count)
    all_kv = spread(spread_even(kv))
    key_place = jnp.concatenate([(time_place ^ other) * shard_tokens + within for other in order])
    place_in, counts = shard_count(key_place, valid_counts, shard_tokens)
    key_real = (place_in * 4 < counts).astype(jnp.int32)
    attended = attend(
        query_chunks, all_kv, scale, cosine, sine, own_place[:, None], key_place[None, :],
        key_real[None, :], key_cols // HDIM,
    )
    return (conf_out, attended)


def solution(mesh):
    placed = (
        P(("tm", "mp"), None),
        P(),
        P(),
        P(),
        P(),
        P(),
        P(),
        P(),
        P(),
        P(),
        P("tm", "mp"),
        P(),
        P("tm", "mp"),
        P("tm", "mp"),
        P("tm", "mp"),
    )
    return jax.shard_map(
        on_device,
        mesh=mesh,
        in_specs=placed,
        out_specs=(P(("tm", "mp"), None), P("tm", "mp")),
        check_vma=False,
    )
```

```python
import jax
import jax.numpy as jnp
from jax import lax
from jax.experimental import pallas as pl
from jax.experimental.pallas import tpu as pltpu
from jax.sharding import PartitionSpec as P

CH = 16
HDIM = 128
SPAN = 40


eps_conf = 1e-05
eps_llm = 1e-06
rope_base = 1000000.0
masked_score = -1e30


def shifted(value, axis, by):
    length = lax.axis_size(axis)
    return lax.ppermute(value, axis, [(i, i + by) for i in range(length - by)])


def swapped(value, bits):
    length = lax.axis_size("tm")
    return lax.ppermute(value, "tm", [(i, i ^ bits) for i in range(length)])


def rotated(value, by):
    length = lax.axis_size("mp")
    return lax.ppermute(value, "mp", [(i, (i + by) % length) for i in range(length)])


def shard_count(index, valid_counts, shard_len):
    shard = index // shard_len
    table = jnp.arange(valid_counts.shape[0], dtype=jnp.int32)
    hit = shard[:, None] == table[None, :]
    count = jnp.sum(jnp.where(hit, valid_counts[None, :], 0), axis=1)
    return (index - shard * shard_len, count)


def layer_norm(field, gain):
    center = field - jnp.mean(field, axis=-1, keepdims=True)
    spread = jnp.mean(center * center, axis=-1, keepdims=True)
    return center * lax.rsqrt(spread + eps_conf) * gain


def rotary_tables(positions, size):
    half = size // 2
    freq = rope_base ** (-(jnp.arange(half, dtype=jnp.float32) * 2.0) / size)
    angle = positions.astype(jnp.float32)[:, None] * freq[None, :]
    cosine = jnp.concatenate([jnp.cos(angle), jnp.cos(angle)], axis=-1)
    sine = jnp.concatenate([-jnp.sin(angle), jnp.sin(angle)], axis=-1)
    return cosine, sine


def turn(field, cosine, sine):
    return field * cosine + pltpu.roll(field, HDIM // 2, 1) * sine


def total_of(refs, columns):
    parts = [ref[:, columns].astype(jnp.float32) for ref in refs]
    while len(parts) > 1:
        parts = [sum(parts[i : i + 2]) for i in range(0, len(parts), 2)]
    return parts[0]


def finish_keys(parts, cosine, sine, key_cols, width):
    rows = cosine.shape[0]

    def kernel(*refs):
        part_refs, (cos_ref, sin_ref, kv_ref, scale_ref) = refs[: len(parts)], refs[len(parts) :]
        squares = total_of(part_refs, pl.ds(2 * key_cols, HDIM))
        power = (
            squares[:, 0:1] + squares[:, 32:33] + squares[:, 64:65] + squares[:, 96:97]
        ) * (1.0 / width)
        scale = lax.rsqrt(power + eps_llm)
        scale_ref[...] = jnp.broadcast_to(scale, scale_ref.shape)
        for head in range(key_cols // HDIM):
            columns = pl.ds(head * HDIM, HDIM)
            raw = total_of(part_refs, columns) * scale
            kv_ref[:, columns] = turn(raw, cos_ref[...], sin_ref[...]).astype(jnp.bfloat16)
        columns = pl.ds(key_cols, key_cols)
        kv_ref[:, columns] = (total_of(part_refs, columns) * scale).astype(jnp.bfloat16)

    return pl.pallas_call(
        kernel,
        out_shape=(
            jax.ShapeDtypeStruct((rows, 2 * key_cols), jnp.bfloat16),
            jax.ShapeDtypeStruct((rows, HDIM), jnp.float32),
        ),
        name="finish_keys",
    )(*parts, cosine, sine)


def attend(chunks, kv, scale, cosine, sine, query_place, key_place, key_real, kv_heads):
    count, each = len(chunks), len(chunks[0])
    rows, chunk_cols = chunks[0][0].shape
    tokens = kv.shape[0]
    chunk_heads = chunk_cols // HDIM
    group = count * chunk_heads // kv_heads
    step = 2 if chunk_heads % 2 == 0 and tokens <= 2048 else 1
    factor = HDIM**-0.5

    def kernel(*refs):
        part_refs = refs[: count * each]
        scale_ref, cos_ref, sin_ref, at_ref, place_ref, real_ref, kv_ref, out_ref = refs[count * each :]
        at, place = at_ref[...], place_ref[...]
        seen = (place <= at) & ((real_ref[...] > 0) | (place == at))
        bias = jnp.where(seen, 0.0, masked_score)
        bias = jnp.concatenate([bias] * step, axis=0)
        for first in range(0, count * chunk_heads, step):
            refs_here = part_refs[first // chunk_heads * each : (first // chunk_heads + 1) * each]
            kv_head = first // group
            queries = []
            for head in range(first % chunk_heads, first % chunk_heads + step):
                raw = total_of(refs_here, pl.ds(head * HDIM, HDIM)) * scale_ref[...]
                queries.append(turn(raw, cos_ref[...], sin_ref[...]).astype(jnp.bfloat16))
            scores = lax.dot_general(
                jnp.concatenate(queries, axis=0),
                kv_ref[:, pl.ds(kv_head * HDIM, HDIM)],
                (((1,), (1,)), ((), ())),
                preferred_element_type=jnp.float32,
            )
            scores = scores * factor + bias
            top = jnp.max(scores, axis=-1, keepdims=True)
            weights = jnp.exp(scores - top)
            total = jnp.sum(weights, axis=-1, keepdims=True)
            summed = jnp.dot(
                weights.astype(jnp.bfloat16),
                kv_ref[:, pl.ds((kv_heads + kv_head) * HDIM, HDIM)],
                preferred_element_type=jnp.float32,
            )
            result = (summed / total).astype(jnp.bfloat16)
            for i in range(step):
                out_ref[:, pl.ds((first + i) * HDIM, HDIM)] = result[i * rows : (i + 1) * rows]

    flat = [part for chunk in chunks for part in chunk]
    return pl.pallas_call(
        kernel,
        out_shape=jax.ShapeDtypeStruct((rows, count * chunk_cols), jnp.bfloat16),
        compiler_params=pltpu.CompilerParams(vmem_limit_bytes=(16 << 20) * max(1, tokens // 2048)),
        name="attend",
    )(*flat, scale, cosine, sine, query_place, key_place, key_real, kv)


def project(held, gain, w_qkv):
    rows, width = held.shape
    wide = w_qkv.shape[1]
    step = width

    def kernel(held_ref, gain_ref, weight_ref, out_ref, normed_ref):
        @pl.when(pl.program_id(0) == 0)
        def _():
            normed_ref[...] = layer_norm(held_ref[...].astype(jnp.float32), gain_ref[...]).astype(
                jnp.bfloat16
            )

        out_ref[...] = jnp.dot(
            normed_ref[...], weight_ref[...], preferred_element_type=jnp.float32
        ).astype(jnp.bfloat16)

    return pl.pallas_call(
        kernel,
        grid=(wide // step,),
        in_specs=[
            pl.BlockSpec((rows, width), lambda i: (0, 0)),
            pl.BlockSpec((1, width), lambda i: (0, 0)),
            pl.BlockSpec((width, step), lambda i: (0, i)),
        ],
        out_specs=pl.BlockSpec((rows, step), lambda i: (0, i)),
        out_shape=jax.ShapeDtypeStruct((rows, wide), jnp.bfloat16),
        scratch_shapes=[pltpu.VMEM((rows, width), jnp.bfloat16)],
        compiler_params=pltpu.CompilerParams(vmem_limit_bytes=12 << 20),
        cost_estimate=pl.CostEstimate(
            flops=2 * rows * width * wide, bytes_accessed=2 * width * wide, transcendentals=0
        ),
        name="project",
    )(held, gain[None, :], w_qkv)


def gate_frames(
    frames, own_proj, near_proj, key_row, query_col, w_attn_out, norm_conv, w_point_in, tail_rows
):
    frame_rows, width = frames.shape
    near_rows = near_proj.shape[0]
    key_rows = near_rows + frame_rows
    head_size = width // CH
    lanes = 2 * head_size

    def kernel(
        frames_ref, own_ref, near_ref, key_row_ref, query_col_ref, gain_ref, attn_hbm, in_hbm,
        mid_ref, glu_ref, tail_ref, attn_w, in_w, context_ref, sems,
    ):
        copies = [
            pltpu.make_async_copy(attn_hbm, attn_w, sems.at[0]),
            pltpu.make_async_copy(in_hbm, in_w, sems.at[1]),
        ]
        for copy in copies:
            copy.start()
        key_at, key_id, key_live = key_row_ref[0:1], key_row_ref[1:2], key_row_ref[2:3]
        at, ids, live = query_col_ref[:, 0:1], query_col_ref[:, 1:2], query_col_ref[:, 2:3]
        seen = (key_at <= at) & (key_id >= ids - 2) & ((key_live > 0) | (key_at == at))
        bias = jnp.where(seen, 0.0, masked_score)
        bias = jnp.concatenate([bias, bias], axis=0)
        left = lax.broadcasted_iota(jnp.int32, (frame_rows, lanes), 1) < head_size
        for pair in range(width // lanes):

            def both_rows(offset):
                columns = pl.ds(offset + pair * lanes, lanes)
                return jnp.concatenate([near_ref[:, columns], own_ref[:, columns]], axis=0)

            query = own_ref[:, pl.ds(pair * lanes, lanes)]
            none = jnp.zeros_like(query)
            query = jnp.concatenate(
                [jnp.where(left, query, none), jnp.where(left, none, query)], axis=0
            )
            scores = lax.dot_general(
                query, both_rows(width), (((1,), (1,)), ((), ())), preferred_element_type=jnp.float32
            )
            scores = scores * head_size**-0.5 + bias
            top = jnp.max(scores, axis=-1, keepdims=True)
            weights = jnp.exp(scores - top)
            total = jnp.sum(weights, axis=-1, keepdims=True)
            summed = jnp.dot(
                weights.astype(jnp.bfloat16), both_rows(2 * width), preferred_element_type=jnp.float32
            )
            context = summed / total
            context_ref[:, pl.ds(pair * lanes, lanes)] = jnp.where(
                left, context[:frame_rows], context[frame_rows:]
            ).astype(jnp.bfloat16)
        copies[0].wait()
        mid = frames_ref[...].astype(jnp.float32) + jnp.dot(
            context_ref[...], attn_w[...], preferred_element_type=jnp.float32
        )
        mid_ref[...] = mid
        conv_in = layer_norm(mid, gain_ref[...]).astype(jnp.bfloat16)
        copies[1].wait()
        part = 256
        for start in range(0, width, part):
            value = jnp.dot(
                conv_in, in_w[:, pl.ds(start, part)], preferred_element_type=jnp.float32
            )
            gate = jnp.dot(
                conv_in, in_w[:, pl.ds(width + start, part)], preferred_element_type=jnp.float32
            )
            glu = jnp.where(live > 0, value * jax.nn.sigmoid(gate), 0.0).astype(jnp.bfloat16)
            glu_ref[:, pl.ds(start, part)] = glu
            tail_ref[:, pl.ds(start, part)] = glu[frame_rows - tail_rows :]

    plain = pl.BlockSpec(memory_space=pltpu.VMEM)
    apart = pl.BlockSpec(memory_space=pl.ANY)
    return pl.pallas_call(
        kernel,
        in_specs=[plain] * 6 + [apart] * 2,
        out_specs=(plain, plain, plain),
        out_shape=(
            jax.ShapeDtypeStruct((frame_rows, width), jnp.float32),
            jax.ShapeDtypeStruct((frame_rows, width), jnp.bfloat16),
            jax.ShapeDtypeStruct((tail_rows, width), jnp.bfloat16),
        ),
        scratch_shapes=[
            pltpu.VMEM(w_attn_out.shape, jnp.bfloat16),
            pltpu.VMEM(w_point_in.shape, jnp.bfloat16),
            pltpu.VMEM((frame_rows, width), jnp.bfloat16),
            pltpu.SemaphoreType.DMA((2,)),
        ],
        compiler_params=pltpu.CompilerParams(vmem_limit_bytes=16 << 20),
        cost_estimate=pl.CostEstimate(
            flops=2 * frame_rows * width * 3 * width,
            bytes_accessed=6 * width * width,
            transcendentals=CH * frame_rows * key_rows,
        ),
        name="gate_frames",
    )(
        frames, own_proj, near_proj, key_row, query_col, norm_conv[None, :], w_attn_out, w_point_in
    )


def finish_frames(mid, glu, rim, real_col, depth_weights, w_point_out):
    frame_rows, width = mid.shape
    extra = rim.shape[0]
    pooled_rows = frame_rows // 4
    taps = depth_weights.shape[0]

    def kernel(
        mid_ref, glu_ref, rim_ref, real_ref, depth_ref, out_ref, conf_ref, pooled_ref, held_ref,
        active_ref,
    ):
        held_ref[:extra] = rim_ref[...].astype(jnp.float32)
        held_ref[extra:] = glu_ref[...].astype(jnp.float32)
        for start in range(0, width, 128):
            columns = pl.ds(start, 128)
            depth = jnp.zeros((frame_rows, 128), jnp.float32)
            for tap in range(taps):
                depth = depth + depth_ref[tap : tap + 1, columns] * held_ref[
                    pl.ds(extra - tap, frame_rows), columns
                ]
            active_ref[:, columns] = jax.nn.silu(depth).astype(jnp.bfloat16)
        final = mid_ref[...] + jnp.dot(
            active_ref[...], out_ref[...], preferred_element_type=jnp.float32
        )
        conf = jnp.where(real_ref[...] > 0, final, 0.0).astype(jnp.bfloat16)
        conf_ref[...] = conf
        row = lax.broadcasted_iota(jnp.int32, (pooled_rows, frame_rows), 0)
        column = lax.broadcasted_iota(jnp.int32, (pooled_rows, frame_rows), 1)
        mean = jnp.where(column // 4 == row, 0.25, 0.0).astype(jnp.bfloat16)
        pooled_ref[...] = jnp.dot(mean, conf, preferred_element_type=jnp.float32).astype(
            jnp.bfloat16
        )

    return pl.pallas_call(
        kernel,
        out_shape=(
            jax.ShapeDtypeStruct((frame_rows, width), jnp.bfloat16),
            jax.ShapeDtypeStruct((pooled_rows, width), jnp.bfloat16),
        ),
        scratch_shapes=[
            pltpu.VMEM((extra + frame_rows, width), jnp.float32),
            pltpu.VMEM((frame_rows, width), jnp.bfloat16),
        ],
        compiler_params=pltpu.CompilerParams(vmem_limit_bytes=8 << 20),
        cost_estimate=pl.CostEstimate(
            flops=2 * frame_rows * width * width, bytes_accessed=2 * width * width, transcendentals=0
        ),
        name="finish_frames",
    )(mid, glu, rim, real_col, depth_weights, w_point_out)


def conformer(
    frames, own_proj, near, first, block_ids, valid_counts, shard_frames, norm_attn, w_qkv,
    w_attn_out, norm_conv, w_point_in, depth_weights, w_point_out,
):
    before = near.shape[0]
    key_rows = before + frames.shape[0]
    near_proj = project(near, norm_attn, w_qkv)
    key_index = first - before + jnp.arange(key_rows, dtype=jnp.int32)
    key_place, key_count = shard_count(key_index, valid_counts, shard_frames)
    key_real = (key_place < key_count) & (key_index >= 0)
    padded_ids = jnp.concatenate([jnp.full((before,), -100, jnp.int32), block_ids])
    key_ids = lax.dynamic_slice_in_dim(padded_ids, first, key_rows, 0)
    key_row = jnp.stack([key_index, key_ids, key_real.astype(jnp.int32)])
    query_col = jnp.transpose(key_row[:, before:])
    mid, glu, tail = gate_frames(
        frames, own_proj, near_proj, key_row, query_col, w_attn_out, norm_conv, w_point_in, 32
    )
    rim = shifted(tail, ("tm", "mp"), 1)
    return finish_frames(mid, glu, rim, query_col[:, 2:3], depth_weights, w_point_out)


def line_pieces(value, beside):
    mp_count, place = lax.axis_size("mp"), lax.axis_index("mp")
    if mp_count != 4:
        pieces = [value] + [rotated(value, by) for by in range(1, mp_count)]
        return [jnp.stack(pieces)], lambda source: (place - source) % mp_count, beside
    below = lax.ppermute(value, "mp", [(0, 1), (1, 2), (2, 3)])
    above = lax.ppermute(value, "mp", [(1, 0), (2, 1), (3, 2)])
    half = value.shape[0] // 2
    own, below, above, beside = lax.optimization_barrier(
        ((value[:half], value[half:]), below, above, beside)
    )
    chunks, waiting = [], (own, below, above)
    for start in (0, half):
        own, below, above = waiting
        mine, lower, upper = own[start // half], below[start : start + half], above[start : start + half]
        far = lax.ppermute(mine, "mp", [(0, 3), (3, 0)])
        lower_2 = lax.ppermute(lower, "mp", [(1, 2), (2, 3)])
        upper_2 = lax.ppermute(upper, "mp", [(2, 1), (1, 0)])
        if start == 0:
            far, lower_2, upper_2, waiting = lax.optimization_barrier(
                (far, lower_2, upper_2, waiting)
            )
        chunks.append(jnp.stack([far, lower_2, lower, mine, upper, upper_2]))
    return chunks, lambda source: (source - place + 3) % 6, beside


def chip_adapter_columns(stacked, row_of):
    tm_count = lax.axis_size("tm")
    time_place = lax.axis_index("tm")
    kept = []
    for other in range(0, tm_count, 2):
        wanted = (time_place ^ other) // 2
        piece = lax.dynamic_index_in_dim(stacked, row_of(wanted), 0, keepdims=False)
        kept.append(swapped(piece, other) if other else piece)
    return kept


def adapt(pooled, near, gain):
    tm_count, time_place = lax.axis_size("tm"), lax.axis_index("tm")
    part, cols = near[0][0].shape
    half = cols // 2
    tokens, depth = pooled.shape
    flat = [array for chunk in near for array in chunk]
    place_word = time_place.reshape(1).astype(jnp.int32)
    plain = pl.BlockSpec(memory_space=pltpu.VMEM)
    scalar = pl.BlockSpec(memory_space=pltpu.SMEM)

    def halves(place_ref, *refs):
        for away, out_ref in enumerate(refs[-2:]):
            columns = pl.ds(pl.multiple_of((place_ref[0] + away) % 2 * half, 128), half)
            for i, ref in enumerate(refs[:-2]):
                out_ref[i * part : (i + 1) * part, :] = ref[:, columns]

    mine, given = pl.pallas_call(
        halves,
        in_specs=[scalar] + [plain] * len(flat),
        out_specs=(plain, plain),
        out_shape=(jax.ShapeDtypeStruct((len(flat) * part, half), jnp.bfloat16),) * 2,
        compiler_params=pltpu.CompilerParams(vmem_limit_bytes=4 << 20),
        name="halves",
    )(place_word, *flat)
    taken = swapped(given, 1)
    step = min(256, tokens)

    def kernel(
        place_ref, mine_ref, taken_ref, pooled_ref, gain_ref, out_ref, word_ref, weight_ref
    ):
        place = place_ref[0]
        for i in range(len(flat)):
            chunk, other = i // (tm_count // 2), 2 * (i % (tm_count // 2))
            for shift, ref in enumerate((mine_ref, taken_ref)):
                source = place ^ (other + shift)
                row = pl.multiple_of(source * (part * len(near)) + chunk * part, part)
                weight_ref[pl.ds(row, part), :] = ref[i * part : (i + 1) * part]
        lane = lax.broadcasted_iota(jnp.int32, (step, HDIM), 1) // 32 - 2 * (place % 2)
        for start in range(0, tokens, step):
            rows = pl.ds(start, step)
            adapted = jnp.dot(
                pooled_ref[rows, :], weight_ref[...], preferred_element_type=jnp.float32
            )
            out_ref[rows, :] = (adapted * gain_ref[...]).astype(jnp.bfloat16)
            squares = jnp.sum(adapted * adapted, axis=-1, keepdims=True)
            high = squares.astype(jnp.bfloat16).astype(jnp.float32)
            words = jnp.where(lane == 0, high, jnp.where(lane == 1, squares - high, 0.0))
            word_ref[rows, :] = words.astype(jnp.bfloat16)

    return pl.pallas_call(
        kernel,
        in_specs=[scalar] + [plain] * 4,
        out_specs=(plain, plain),
        out_shape=(
            jax.ShapeDtypeStruct((tokens, half), jnp.bfloat16),
            jax.ShapeDtypeStruct((tokens, HDIM), jnp.bfloat16),
        ),
        scratch_shapes=[pltpu.VMEM((depth, half), jnp.bfloat16)],
        compiler_params=pltpu.CompilerParams(vmem_limit_bytes=16 << 20),
        name="adapt",
    )(place_word, mine, taken, pooled, gain[None, :])


def spread_even(value):
    tm_count = lax.axis_size("tm")
    blocks = [value] + [swapped(value, other) for other in range(2, tm_count, 2)]
    return jnp.concatenate(blocks, axis=0)


def spread(even):
    return jnp.concatenate([even, swapped(even, 1)], axis=0)


def both_sum(one, other):
    return (one.astype(jnp.float32) + other.astype(jnp.float32)).astype(jnp.bfloat16)


def direct_parts(value):
    tm_count = lax.axis_size("tm")
    half = value.shape[0] // 2
    rows = value.shape[0] // tm_count
    chip = both_sum(value[:half], swapped(value[half:], 1))
    return [chip[:rows]] + [
        swapped(chip[i * rows : (i + 1) * rows], 2 * i) for i in range(1, tm_count // 2)
    ]


def chip_sum(left, right, weight):
    def product(rows):
        return jnp.dot(rows, weight, preferred_element_type=jnp.float32)

    other = swapped(product(right).astype(jnp.bfloat16), 1)
    return (product(left) + other.astype(jnp.float32)).astype(jnp.bfloat16)


def halved(held, bit, axes):
    axis = axes.index(bit)
    keep = lax.index_in_dim(held, 0, axis, keepdims=False)
    given = lax.index_in_dim(held, 1, axis, keepdims=False)
    return keep, swapped(given, 2 << bit), axes[:axis] + axes[axis + 1 :]


def on_device(
    frames,
    block_ids,
    valid_counts,
    norm_attn,
    w_qkv,
    w_attn_out,
    norm_conv,
    w_point_in,
    w_depth,
    w_point_out,
    w_adapter,
    llm_gain,
    w_query,
    w_key,
    w_value,
):
    tm_count, mp_count = lax.axis_size("tm"), lax.axis_size("mp")
    time_place, model_place = lax.axis_index("tm"), lax.axis_index("mp")
    frame_rows, width = frames.shape
    shard_frames = frame_rows * mp_count
    first = (time_place * mp_count + model_place) * frame_rows
    near = shifted(frames, ("tm", "mp"), 1)
    own_proj = project(frames, norm_attn, w_qkv)
    depth_weights = w_depth.astype(jnp.float32)
    w_adapter, own_proj = lax.optimization_barrier((w_adapter, own_proj))
    conf_out, pooled = conformer(
        frames, own_proj, near, first, block_ids, valid_counts, shard_frames, norm_attn, w_qkv,
        w_attn_out, norm_conv, w_point_in, depth_weights, w_point_out,
    )
    stacked, row_of, pooled = line_pieces(w_adapter, pooled)
    piece = pooled.shape[0]
    shard_tokens = piece * mp_count
    cycle = [rotated(pooled, by) for by in range(mp_count - 1, 0, -1)] + [pooled]
    shard_pooled = lax.dynamic_slice_in_dim(
        jnp.concatenate(cycle + cycle, axis=0), (mp_count - 1 - model_place) * piece, shard_tokens, 0
    )
    even_pooled, stacked[0] = lax.optimization_barrier((spread_even(shard_pooled), stacked[0]))
    all_pooled, near_columns = lax.optimization_barrier(
        (
            spread(even_pooled),
            [chip_adapter_columns(chunk, row_of) for chunk in stacked],
        )
    )
    tokens = all_pooled.shape[0]
    block = w_adapter.shape[1] * mp_count // tm_count
    gain = lax.dynamic_slice_in_dim(llm_gain, time_place * block, block, 0)
    scaled, words = adapt(all_pooled, near_columns, gain)
    raw_keys = jnp.dot(scaled, w_key, preferred_element_type=jnp.float32).astype(jnp.bfloat16)
    raw_values = jnp.dot(scaled, w_value, preferred_element_type=jnp.float32).astype(jnp.bfloat16)
    key_cols, half_cols = w_key.shape[1], w_query.shape[1] // 2
    kv_raw, scaled = lax.optimization_barrier(
        (jnp.concatenate([raw_keys, raw_values, words], axis=1), scaled)
    )
    kv_parts = direct_parts(kv_raw)
    bits = list(range(tm_count.bit_length() - 2))
    left, right = scaled[: tokens // 2], scaled[tokens // 2 :]
    sums = [
        chip_sum(left, right, w_query[:, :half_cols]),
        chip_sum(left, right, w_query[:, half_cols:]),
    ]
    kv_parts, _ = lax.optimization_barrier((kv_parts, sums))
    query_chunks, rest = [], [bits, bits[::-1]]
    for held, turns in zip(sums, rest):
        held = held.reshape((2,) * len(bits) + (shard_tokens, half_cols))
        keep, taken, left_axes = halved(held, turns[0], bits[::-1])
        for turn_bit in turns[1:]:
            keep, taken, left_axes = halved(both_sum(keep, taken), turn_bit, left_axes)
        query_chunks.append((keep, taken))
    order = list(range(0, tm_count, 2)) + list(range(1, tm_count, 2))
    within = jnp.arange(shard_tokens, dtype=jnp.int32)
    own_place = time_place * shard_tokens + within
    cosine, sine = rotary_tables(own_place, HDIM)
    kv, scale = finish_keys(kv_parts, cosine, sine, key_cols, block * tm_count)
    all_kv = spread(spread_even(kv))
    key_place = jnp.concatenate([(time_place ^ other) * shard_tokens + within for other in order])
    place_in, counts = shard_count(key_place, valid_counts, shard_tokens)
    key_real = (place_in * 4 < counts).astype(jnp.int32)
    attended = attend(
        query_chunks, all_kv, scale, cosine, sine, own_place[:, None], key_place[None, :],
        key_real[None, :], key_cols // HDIM,
    )
    return (conf_out, attended)


def solution(mesh):
    placed = (
        P(("tm", "mp"), None),
        P(),
        P(),
        P(),
        P(),
        P(),
        P(),
        P(),
        P(),
        P(),
        P("tm", "mp"),
        P(),
        P("tm", "mp"),
        P("tm", "mp"),
        P("tm", "mp"),
    )
    return jax.shard_map(
        on_device,
        mesh=mesh,
        in_specs=placed,
        out_specs=(P(("tm", "mp"), None), P("tm", "mp")),
        check_vma=False,
    )
```

```python
import jax
import jax.numpy as jnp
from jax import lax
from jax.experimental import pallas as pl
from jax.experimental.pallas import tpu as pltpu
from jax.sharding import PartitionSpec as P

CH = 16
HDIM = 128
SPAN = 40


eps_conf = 1e-05
eps_llm = 1e-06
rope_base = 1000000.0
masked_score = -1e30


def shifted(value, axis, by):
    length = lax.axis_size(axis)
    return lax.ppermute(value, axis, [(i, i + by) for i in range(length - by)])


def swapped(value, bits):
    length = lax.axis_size("tm")
    return lax.ppermute(value, "tm", [(i, i ^ bits) for i in range(length)])


def rotated(value, by):
    length = lax.axis_size("mp")
    return lax.ppermute(value, "mp", [(i, (i + by) % length) for i in range(length)])


def shard_count(index, valid_counts, shard_len):
    shard = index // shard_len
    table = jnp.arange(valid_counts.shape[0], dtype=jnp.int32)
    hit = shard[:, None] == table[None, :]
    count = jnp.sum(jnp.where(hit, valid_counts[None, :], 0), axis=1)
    return (index - shard * shard_len, count)


def layer_norm(field, gain):
    center = field - jnp.mean(field, axis=-1, keepdims=True)
    spread = jnp.mean(center * center, axis=-1, keepdims=True)
    return center * lax.rsqrt(spread + eps_conf) * gain


def rotary_tables(positions, size):
    half = size // 2
    freq = rope_base ** (-(jnp.arange(half, dtype=jnp.float32) * 2.0) / size)
    angle = positions.astype(jnp.float32)[:, None] * freq[None, :]
    cosine = jnp.concatenate([jnp.cos(angle), jnp.cos(angle)], axis=-1)
    sine = jnp.concatenate([-jnp.sin(angle), jnp.sin(angle)], axis=-1)
    return cosine, sine


def turn(field, cosine, sine):
    return field * cosine + pltpu.roll(field, HDIM // 2, 1) * sine


def total_of(refs, columns):
    parts = [ref[:, columns].astype(jnp.float32) for ref in refs]
    while len(parts) > 1:
        parts = [sum(parts[i : i + 2]) for i in range(0, len(parts), 2)]
    return parts[0]


def finish_keys(parts, cosine, sine, key_cols, width):
    rows = cosine.shape[0]

    def kernel(*refs):
        part_refs, (cos_ref, sin_ref, kv_ref, scale_ref) = refs[: len(parts)], refs[len(parts) :]
        squares = total_of(part_refs, pl.ds(2 * key_cols, HDIM))
        power = (
            squares[:, 0:1] + squares[:, 32:33] + squares[:, 64:65] + squares[:, 96:97]
        ) * (1.0 / width)
        scale = lax.rsqrt(power + eps_llm)
        scale_ref[...] = jnp.broadcast_to(scale, scale_ref.shape)
        for head in range(key_cols // HDIM):
            columns = pl.ds(head * HDIM, HDIM)
            raw = total_of(part_refs, columns) * scale
            kv_ref[:, columns] = turn(raw, cos_ref[...], sin_ref[...]).astype(jnp.bfloat16)
        columns = pl.ds(key_cols, key_cols)
        kv_ref[:, columns] = (total_of(part_refs, columns) * scale).astype(jnp.bfloat16)

    return pl.pallas_call(
        kernel,
        out_shape=(
            jax.ShapeDtypeStruct((rows, 2 * key_cols), jnp.bfloat16),
            jax.ShapeDtypeStruct((rows, HDIM), jnp.float32),
        ),
        name="finish_keys",
    )(*parts, cosine, sine)


def attend(chunks, kv, scale, cosine, sine, query_place, key_place, key_real, kv_heads):
    count, each = len(chunks), len(chunks[0])
    rows, chunk_cols = chunks[0][0].shape
    tokens = kv.shape[0]
    chunk_heads = chunk_cols // HDIM
    group = count * chunk_heads // kv_heads
    step = 2 if chunk_heads % 2 == 0 and tokens <= 2048 else 1
    factor = HDIM**-0.5

    def kernel(*refs):
        part_refs = refs[: count * each]
        scale_ref, cos_ref, sin_ref, at_ref, place_ref, real_ref, kv_ref, out_ref = refs[count * each :]
        at, place = at_ref[...], place_ref[...]
        seen = (place <= at) & ((real_ref[...] > 0) | (place == at))
        bias = jnp.where(seen, 0.0, masked_score)
        bias = jnp.concatenate([bias] * step, axis=0)
        for first in range(0, count * chunk_heads, step):
            refs_here = part_refs[first // chunk_heads * each : (first // chunk_heads + 1) * each]
            kv_head = first // group
            queries = []
            for head in range(first % chunk_heads, first % chunk_heads + step):
                raw = total_of(refs_here, pl.ds(head * HDIM, HDIM)) * scale_ref[...]
                queries.append(turn(raw, cos_ref[...], sin_ref[...]).astype(jnp.bfloat16))
            scores = lax.dot_general(
                jnp.concatenate(queries, axis=0),
                kv_ref[:, pl.ds(kv_head * HDIM, HDIM)],
                (((1,), (1,)), ((), ())),
                preferred_element_type=jnp.float32,
            )
            scores = scores * factor + bias
            top = jnp.max(scores, axis=-1, keepdims=True)
            weights = jnp.exp(scores - top)
            total = jnp.sum(weights, axis=-1, keepdims=True)
            summed = jnp.dot(
                weights.astype(jnp.bfloat16),
                kv_ref[:, pl.ds((kv_heads + kv_head) * HDIM, HDIM)],
                preferred_element_type=jnp.float32,
            )
            result = (summed / total).astype(jnp.bfloat16)
            for i in range(step):
                out_ref[:, pl.ds((first + i) * HDIM, HDIM)] = result[i * rows : (i + 1) * rows]

    flat = [part for chunk in chunks for part in chunk]
    return pl.pallas_call(
        kernel,
        out_shape=jax.ShapeDtypeStruct((rows, count * chunk_cols), jnp.bfloat16),
        compiler_params=pltpu.CompilerParams(vmem_limit_bytes=(16 << 20) * max(1, tokens // 2048)),
        name="attend",
    )(*flat, scale, cosine, sine, query_place, key_place, key_real, kv)


def project(near, frames, gain, w_qkv):
    rows, width = frames.shape
    both = near.shape[0] + rows
    wide = w_qkv.shape[1]

    def kernel(near_ref, frames_ref, gain_ref, weight_ref, out_ref):
        held = jnp.concatenate([near_ref[...], frames_ref[...]], axis=0).astype(jnp.float32)
        normed = layer_norm(held, gain_ref[...]).astype(jnp.bfloat16)
        for start in range(0, wide, width):
            columns = pl.ds(start, width)
            out_ref[:, columns] = jnp.dot(
                normed, weight_ref[:, columns], preferred_element_type=jnp.float32
            ).astype(jnp.bfloat16)

    return pl.pallas_call(
        kernel,
        out_shape=jax.ShapeDtypeStruct((both, wide), jnp.bfloat16),
        compiler_params=pltpu.CompilerParams(vmem_limit_bytes=16 << 20),
        cost_estimate=pl.CostEstimate(
            flops=2 * both * width * wide, bytes_accessed=2 * width * wide, transcendentals=0
        ),
        name="project",
    )(near, frames, gain[None, :], w_qkv)


def gate_frames(
    frames, proj, key_row, query_col, w_attn_out, norm_conv, w_point_in, tail_rows
):
    frame_rows, width = frames.shape
    key_rows = proj.shape[0]
    head_size = width // CH
    lanes = 2 * head_size

    def kernel(
        frames_ref, proj_ref, key_row_ref, query_col_ref, gain_ref, attn_hbm, in_hbm,
        mid_ref, glu_ref, tail_ref, attn_w, in_w, context_ref, sems,
    ):
        copies = [
            pltpu.make_async_copy(attn_hbm, attn_w, sems.at[0]),
            pltpu.make_async_copy(in_hbm, in_w, sems.at[1]),
        ]
        for copy in copies:
            copy.start()
        key_at, key_id, key_live = key_row_ref[0:1], key_row_ref[1:2], key_row_ref[2:3]
        at, ids, live = query_col_ref[:, 0:1], query_col_ref[:, 1:2], query_col_ref[:, 2:3]
        seen = (key_at <= at) & (key_id >= ids - 2) & ((key_live > 0) | (key_at == at))
        bias = jnp.where(seen, 0.0, masked_score)
        bias = jnp.concatenate([bias, bias], axis=0)
        left = lax.broadcasted_iota(jnp.int32, (frame_rows, lanes), 1) < head_size
        for pair in range(width // lanes):

            def both_rows(offset):
                columns = pl.ds(offset + pair * lanes, lanes)
                return proj_ref[:, columns]

            query = proj_ref[key_rows - frame_rows :, pl.ds(pair * lanes, lanes)]
            none = jnp.zeros_like(query)
            query = jnp.concatenate(
                [jnp.where(left, query, none), jnp.where(left, none, query)], axis=0
            )
            scores = lax.dot_general(
                query, both_rows(width), (((1,), (1,)), ((), ())), preferred_element_type=jnp.float32
            )
            scores = scores * head_size**-0.5 + bias
            top = jnp.max(scores, axis=-1, keepdims=True)
            weights = jnp.exp(scores - top)
            total = jnp.sum(weights, axis=-1, keepdims=True)
            summed = jnp.dot(
                weights.astype(jnp.bfloat16), both_rows(2 * width), preferred_element_type=jnp.float32
            )
            context = summed / total
            context_ref[:, pl.ds(pair * lanes, lanes)] = jnp.where(
                left, context[:frame_rows], context[frame_rows:]
            ).astype(jnp.bfloat16)
        copies[0].wait()
        mid = frames_ref[...].astype(jnp.float32) + jnp.dot(
            context_ref[...], attn_w[...], preferred_element_type=jnp.float32
        )
        mid_ref[...] = mid
        conv_in = layer_norm(mid, gain_ref[...]).astype(jnp.bfloat16)
        copies[1].wait()
        part = 256
        for start in range(0, width, part):
            value = jnp.dot(
                conv_in, in_w[:, pl.ds(start, part)], preferred_element_type=jnp.float32
            )
            gate = jnp.dot(
                conv_in, in_w[:, pl.ds(width + start, part)], preferred_element_type=jnp.float32
            )
            glu = jnp.where(live > 0, value * jax.nn.sigmoid(gate), 0.0).astype(jnp.bfloat16)
            glu_ref[:, pl.ds(start, part)] = glu
            tail_ref[:, pl.ds(start, part)] = glu[frame_rows - tail_rows :]

    plain = pl.BlockSpec(memory_space=pltpu.VMEM)
    apart = pl.BlockSpec(memory_space=pltpu.HBM)
    return pl.pallas_call(
        kernel,
        in_specs=[plain] * 5 + [apart] * 2,
        out_specs=(plain, plain, plain),
        out_shape=(
            jax.ShapeDtypeStruct((frame_rows, width), jnp.float32),
            jax.ShapeDtypeStruct((frame_rows, width), jnp.bfloat16),
            jax.ShapeDtypeStruct((tail_rows, width), jnp.bfloat16),
        ),
        scratch_shapes=[
            pltpu.VMEM(w_attn_out.shape, jnp.bfloat16),
            pltpu.VMEM(w_point_in.shape, jnp.bfloat16),
            pltpu.VMEM((frame_rows, width), jnp.bfloat16),
            pltpu.SemaphoreType.DMA((2,)),
        ],
        compiler_params=pltpu.CompilerParams(vmem_limit_bytes=16 << 20),
        cost_estimate=pl.CostEstimate(
            flops=2 * frame_rows * width * 3 * width,
            bytes_accessed=6 * width * width,
            transcendentals=CH * frame_rows * key_rows,
        ),
        name="gate_frames",
    )(
        frames, proj, key_row, query_col, norm_conv[None, :], w_attn_out, w_point_in
    )


def convolve_late(glu, depth_weights, extra):
    frame_rows, width = glu.shape
    taps = depth_weights.shape[0]
    late = frame_rows - extra

    def kernel(glu_ref, depth_ref, out_ref, held_ref):
        held_ref[...] = glu_ref[...].astype(jnp.float32)
        for start in range(0, width, 128):
            columns = pl.ds(start, 128)
            depth = jnp.zeros((late, 128), jnp.float32)
            for tap in range(taps):
                depth = depth + depth_ref[tap : tap + 1, columns] * held_ref[
                    pl.ds(extra - tap, late), columns
                ]
            out_ref[:, columns] = jax.nn.silu(depth).astype(jnp.bfloat16)

    return pl.pallas_call(
        kernel,
        out_shape=jax.ShapeDtypeStruct((late, width), jnp.bfloat16),
        scratch_shapes=[pltpu.VMEM((frame_rows, width), jnp.float32)],
        compiler_params=pltpu.CompilerParams(vmem_limit_bytes=8 << 20),
        cost_estimate=pl.CostEstimate(
            flops=2 * taps * late * width, bytes_accessed=4 * late * width, transcendentals=0
        ),
        name="convolve_late",
    )(glu, depth_weights)


def finish_frames(mid, glu, active, rim, real_col, depth_weights, w_point_out):
    frame_rows, width = mid.shape
    extra = rim.shape[0]
    pooled_rows = frame_rows // 4
    taps = depth_weights.shape[0]

    def kernel(
        mid_ref, glu_ref, late_ref, rim_ref, real_ref, depth_ref, out_ref, conf_ref, pooled_ref,
        held_ref, active_ref,
    ):
        held_ref[:extra] = rim_ref[...].astype(jnp.float32)
        held_ref[extra:] = glu_ref[:extra].astype(jnp.float32)
        active_ref[extra:] = late_ref[...]
        for start in range(0, width, 128):
            columns = pl.ds(start, 128)
            depth = jnp.zeros((extra, 128), jnp.float32)
            for tap in range(taps):
                depth = depth + depth_ref[tap : tap + 1, columns] * held_ref[
                    pl.ds(extra - tap, extra), columns
                ]
            active_ref[:extra, columns] = jax.nn.silu(depth).astype(jnp.bfloat16)
        final = mid_ref[...] + jnp.dot(
            active_ref[...], out_ref[...], preferred_element_type=jnp.float32
        )
        conf = jnp.where(real_ref[...] > 0, final, 0.0).astype(jnp.bfloat16)
        conf_ref[...] = conf
        row = lax.broadcasted_iota(jnp.int32, (pooled_rows, frame_rows), 0)
        column = lax.broadcasted_iota(jnp.int32, (pooled_rows, frame_rows), 1)
        mean = jnp.where(column // 4 == row, 0.25, 0.0).astype(jnp.bfloat16)
        pooled_ref[...] = jnp.dot(mean, conf, preferred_element_type=jnp.float32).astype(
            jnp.bfloat16
        )

    return pl.pallas_call(
        kernel,
        out_shape=(
            jax.ShapeDtypeStruct((frame_rows, width), jnp.bfloat16),
            jax.ShapeDtypeStruct((pooled_rows, width), jnp.bfloat16),
        ),
        scratch_shapes=[
            pltpu.VMEM((2 * extra, width), jnp.float32),
            pltpu.VMEM((frame_rows, width), jnp.bfloat16),
        ],
        compiler_params=pltpu.CompilerParams(vmem_limit_bytes=8 << 20),
        cost_estimate=pl.CostEstimate(
            flops=2 * frame_rows * width * width, bytes_accessed=2 * width * width, transcendentals=0
        ),
        name="finish_frames",
    )(mid, glu, active, rim, real_col, depth_weights, w_point_out)


def conformer(
    frames, near, first, block_ids, valid_counts, shard_frames, norm_attn, w_qkv,
    w_attn_out, norm_conv, w_point_in, depth_weights, w_point_out,
):
    before = near.shape[0]
    key_rows = before + frames.shape[0]
    proj = project(near, frames, norm_attn, w_qkv)
    key_index = first - before + jnp.arange(key_rows, dtype=jnp.int32)
    key_place, key_count = shard_count(key_index, valid_counts, shard_frames)
    key_real = (key_place < key_count) & (key_index >= 0)
    padded_ids = jnp.concatenate([jnp.full((before,), -100, jnp.int32), block_ids])
    key_ids = lax.dynamic_slice_in_dim(padded_ids, first, key_rows, 0)
    key_row = jnp.stack([key_index, key_ids, key_real.astype(jnp.int32)])
    query_col = jnp.transpose(key_row[:, before:])
    mid, glu, tail = gate_frames(
        frames, proj, key_row, query_col, w_attn_out, norm_conv, w_point_in, 32
    )
    rim = shifted(tail, ("tm", "mp"), 1)
    active = convolve_late(glu, depth_weights, 32)
    return finish_frames(mid, glu, active, rim, query_col[:, 2:3], depth_weights, w_point_out)


def line_pieces(value, beside):
    mp_count, place = lax.axis_size("mp"), lax.axis_index("mp")
    if mp_count != 4:
        pieces = [value] + [rotated(value, by) for by in range(1, mp_count)]
        return [jnp.stack(pieces)], lambda source: (place - source) % mp_count, beside
    below = lax.ppermute(value, "mp", [(0, 1), (1, 2), (2, 3)])
    above = lax.ppermute(value, "mp", [(1, 0), (2, 1), (3, 2)])
    half = value.shape[0] // 2
    own, below, above, beside = lax.optimization_barrier(
        ((value[:half], value[half:]), below, above, beside)
    )
    chunks, waiting = [], (own, below, above)
    for start in (0, half):
        own, below, above = waiting
        mine, lower, upper = own[start // half], below[start : start + half], above[start : start + half]
        far = lax.ppermute(mine, "mp", [(0, 3), (3, 0)])
        lower_2 = lax.ppermute(lower, "mp", [(1, 2), (2, 3)])
        upper_2 = lax.ppermute(upper, "mp", [(2, 1), (1, 0)])
        if start == 0:
            far, lower_2, upper_2, waiting = lax.optimization_barrier(
                (far, lower_2, upper_2, waiting)
            )
        chunks.append(jnp.stack([far, lower_2, lower, mine, upper, upper_2]))
    return chunks, lambda source: (source - place + 3) % 6, beside


def chip_adapter_columns(stacked, row_of):
    tm_count = lax.axis_size("tm")
    time_place = lax.axis_index("tm")
    kept = []
    for other in range(0, tm_count, 2):
        wanted = (time_place ^ other) // 2
        piece = lax.dynamic_index_in_dim(stacked, row_of(wanted), 0, keepdims=False)
        kept.append(swapped(piece, other) if other else piece)
    return kept


def adapt(pooled, near, gain, w_key, w_value):
    tm_count, time_place = lax.axis_size("tm"), lax.axis_index("tm")
    part, cols = near[0][0].shape
    half = cols // 2
    tokens, depth = pooled.shape
    flat = [array for chunk in near for array in chunk]
    place_word = time_place.reshape(1).astype(jnp.int32)
    plain = pl.BlockSpec(memory_space=pltpu.VMEM)
    scalar = pl.BlockSpec(memory_space=pltpu.SMEM)

    def halves(place_ref, *refs):
        for away, out_ref in enumerate(refs[-2:]):
            columns = pl.ds(pl.multiple_of((place_ref[0] + away) % 2 * half, 128), half)
            for i, ref in enumerate(refs[:-2]):
                out_ref[i * part : (i + 1) * part, :] = ref[:, columns]

    mine, given = pl.pallas_call(
        halves,
        in_specs=[scalar] + [plain] * len(flat),
        out_specs=(plain, plain),
        out_shape=(jax.ShapeDtypeStruct((len(flat) * part, half), jnp.bfloat16),) * 2,
        compiler_params=pltpu.CompilerParams(vmem_limit_bytes=4 << 20),
        name="halves",
    )(place_word, *flat)
    taken = swapped(given, 1)
    step, key_cols = min(256, tokens), w_key.shape[1]

    def kernel(
        place_ref, mine_ref, taken_ref, pooled_ref, gain_ref, key_ref, value_ref, out_ref, kv_ref,
        weight_ref,
    ):
        place = place_ref[0]
        for i in range(len(flat)):
            chunk, other = i // (tm_count // 2), 2 * (i % (tm_count // 2))
            for shift, ref in enumerate((mine_ref, taken_ref)):
                source = place ^ (other + shift)
                row = pl.multiple_of(source * (part * len(near)) + chunk * part, part)
                weight_ref[pl.ds(row, part), :] = ref[i * part : (i + 1) * part]
        lane = lax.broadcasted_iota(jnp.int32, (step, HDIM), 1) // 32 - 2 * (place % 2)
        for start in range(0, tokens, step):
            rows = pl.ds(start, step)
            adapted = jnp.dot(
                pooled_ref[rows, :], weight_ref[...], preferred_element_type=jnp.float32
            )
            scaled = (adapted * gain_ref[...]).astype(jnp.bfloat16)
            out_ref[rows, :] = scaled
            for i, ref in enumerate((key_ref, value_ref)):
                kv_ref[rows, pl.ds(i * key_cols, key_cols)] = jnp.dot(
                    scaled, ref[...], preferred_element_type=jnp.float32
                ).astype(jnp.bfloat16)
            squares = jnp.sum(adapted * adapted, axis=-1, keepdims=True)
            high = squares.astype(jnp.bfloat16).astype(jnp.float32)
            words = jnp.where(lane == 0, high, jnp.where(lane == 1, squares - high, 0.0))
            kv_ref[rows, pl.ds(2 * key_cols, HDIM)] = words.astype(jnp.bfloat16)

    return pl.pallas_call(
        kernel,
        in_specs=[scalar] + [plain] * 6,
        out_specs=(plain, plain),
        out_shape=(
            jax.ShapeDtypeStruct((tokens, half), jnp.bfloat16),
            jax.ShapeDtypeStruct((tokens, 2 * key_cols + HDIM), jnp.bfloat16),
        ),
        scratch_shapes=[pltpu.VMEM((depth, half), jnp.bfloat16)],
        compiler_params=pltpu.CompilerParams(vmem_limit_bytes=18 << 20),
        name="adapt",
    )(place_word, mine, taken, pooled, gain[None, :], w_key, w_value)


def spread_even(value):
    tm_count = lax.axis_size("tm")
    blocks = [value] + [swapped(value, other) for other in range(2, tm_count, 2)]
    return jnp.concatenate(blocks, axis=0)


def spread(even):
    return jnp.concatenate([even, swapped(even, 1)], axis=0)


def both_sum(one, other):
    return (one.astype(jnp.float32) + other.astype(jnp.float32)).astype(jnp.bfloat16)


def direct_parts(value):
    tm_count = lax.axis_size("tm")
    half = value.shape[0] // 2
    rows = value.shape[0] // tm_count
    chip = both_sum(value[:half], swapped(value[half:], 1))
    return [chip[:rows]] + [
        swapped(chip[i * rows : (i + 1) * rows], 2 * i) for i in range(1, tm_count // 2)
    ]


def chip_sum(left, right, weight):
    def product(rows):
        return jnp.dot(rows, weight, preferred_element_type=jnp.float32)

    other = swapped(product(right).astype(jnp.bfloat16), 1)
    return (product(left) + other.astype(jnp.float32)).astype(jnp.bfloat16)


def halved(held, bit, axes):
    axis = axes.index(bit)
    keep = lax.index_in_dim(held, 0, axis, keepdims=False)
    given = lax.index_in_dim(held, 1, axis, keepdims=False)
    return keep, swapped(given, 2 << bit), axes[:axis] + axes[axis + 1 :]


def on_device(
    frames,
    block_ids,
    valid_counts,
    norm_attn,
    w_qkv,
    w_attn_out,
    norm_conv,
    w_point_in,
    w_depth,
    w_point_out,
    w_adapter,
    llm_gain,
    w_query,
    w_key,
    w_value,
):
    tm_count, mp_count = lax.axis_size("tm"), lax.axis_size("mp")
    time_place, model_place = lax.axis_index("tm"), lax.axis_index("mp")
    frame_rows, width = frames.shape
    shard_frames = frame_rows * mp_count
    first = (time_place * mp_count + model_place) * frame_rows
    near = shifted(frames, ("tm", "mp"), 1)
    depth_weights = w_depth.astype(jnp.float32)
    w_adapter, near = lax.optimization_barrier((w_adapter, near))
    conf_out, pooled = conformer(
        frames, near, first, block_ids, valid_counts, shard_frames, norm_attn, w_qkv,
        w_attn_out, norm_conv, w_point_in, depth_weights, w_point_out,
    )
    stacked, row_of, pooled = line_pieces(w_adapter, pooled)
    piece = pooled.shape[0]
    shard_tokens = piece * mp_count
    cycle = [rotated(pooled, by) for by in range(mp_count - 1, 0, -1)] + [pooled]
    shard_pooled = lax.dynamic_slice_in_dim(
        jnp.concatenate(cycle + cycle, axis=0), (mp_count - 1 - model_place) * piece, shard_tokens, 0
    )
    even_pooled, stacked[0] = lax.optimization_barrier((spread_even(shard_pooled), stacked[0]))
    all_pooled, near_columns = lax.optimization_barrier(
        (
            spread(even_pooled),
            [chip_adapter_columns(chunk, row_of) for chunk in stacked],
        )
    )
    tokens = all_pooled.shape[0]
    block = w_adapter.shape[1] * mp_count // tm_count
    gain = lax.dynamic_slice_in_dim(llm_gain, time_place * block, block, 0)
    scaled, kv_raw = adapt(all_pooled, near_columns, gain, w_key, w_value)
    key_cols, half_cols = w_key.shape[1], w_query.shape[1] // 2
    kv_parts = direct_parts(kv_raw)
    bits = list(range(tm_count.bit_length() - 2))
    left, right = scaled[: tokens // 2], scaled[tokens // 2 :]
    sums = [
        chip_sum(left, right, w_query[:, :half_cols]),
        chip_sum(left, right, w_query[:, half_cols:]),
    ]
    kv_parts, _ = lax.optimization_barrier((kv_parts, sums))
    query_chunks, rest = [], [bits, bits[::-1]]
    for held, turns in zip(sums, rest):
        held = held.reshape((2,) * len(bits) + (shard_tokens, half_cols))
        keep, taken, left_axes = halved(held, turns[0], bits[::-1])
        for turn_bit in turns[1:]:
            keep, taken, left_axes = halved(both_sum(keep, taken), turn_bit, left_axes)
        query_chunks.append((keep, taken))
    order = list(range(0, tm_count, 2)) + list(range(1, tm_count, 2))
    within = jnp.arange(shard_tokens, dtype=jnp.int32)
    own_place = time_place * shard_tokens + within
    cosine, sine = rotary_tables(own_place, HDIM)
    kv, scale = finish_keys(kv_parts, cosine, sine, key_cols, block * tm_count)
    all_kv = spread(spread_even(kv))
    key_place = jnp.concatenate([(time_place ^ other) * shard_tokens + within for other in order])
    place_in, counts = shard_count(key_place, valid_counts, shard_tokens)
    key_real = (place_in * 4 < counts).astype(jnp.int32)
    attended = attend(
        query_chunks, all_kv, scale, cosine, sine, own_place[:, None], key_place[None, :],
        key_real[None, :], key_cols // HDIM,
    )
    return (conf_out, attended)


def solution(mesh):
    placed = (
        P(("tm", "mp"), None),
        P(),
        P(),
        P(),
        P(),
        P(),
        P(),
        P(),
        P(),
        P(),
        P("tm", "mp"),
        P(),
        P("tm", "mp"),
        P("tm", "mp"),
        P("tm", "mp"),
    )
    return jax.shard_map(
        on_device,
        mesh=mesh,
        in_specs=placed,
        out_specs=(P(("tm", "mp"), None), P("tm", "mp")),
        check_vma=False,
    )
```

```python
import jax
import jax.numpy as jnp
from jax import lax
from jax.experimental import pallas as pl
from jax.experimental.pallas import tpu as pltpu
from jax.sharding import PartitionSpec as P

CH = 16
HDIM = 128
SPAN = 40


eps_conf = 1e-05
eps_llm = 1e-06
rope_base = 1000000.0
masked_score = -1e30


def shifted(value, axis, by):
    length = lax.axis_size(axis)
    return lax.ppermute(value, axis, [(i, i + by) for i in range(length - by)])


def swapped(value, bits):
    length = lax.axis_size("tm")
    return lax.ppermute(value, "tm", [(i, i ^ bits) for i in range(length)])


def rotated(value, by):
    length = lax.axis_size("mp")
    return lax.ppermute(value, "mp", [(i, (i + by) % length) for i in range(length)])


def shard_count(index, valid_counts, shard_len):
    shard = index // shard_len
    table = jnp.arange(valid_counts.shape[0], dtype=jnp.int32)
    hit = shard[:, None] == table[None, :]
    count = jnp.sum(jnp.where(hit, valid_counts[None, :], 0), axis=1)
    return (index - shard * shard_len, count)


def layer_norm(field, gain):
    center = field - jnp.mean(field, axis=-1, keepdims=True)
    spread = jnp.mean(center * center, axis=-1, keepdims=True)
    return center * lax.rsqrt(spread + eps_conf) * gain


def rotary_tables(positions, size):
    half = size // 2
    freq = rope_base ** (-(jnp.arange(half, dtype=jnp.float32) * 2.0) / size)
    angle = positions.astype(jnp.float32)[:, None] * freq[None, :]
    cosine = jnp.concatenate([jnp.cos(angle), jnp.cos(angle)], axis=-1)
    sine = jnp.concatenate([-jnp.sin(angle), jnp.sin(angle)], axis=-1)
    return cosine, sine


def turn(field, cosine, sine):
    return field * cosine + pltpu.roll(field, HDIM // 2, 1) * sine


def total_of(refs, columns):
    parts = [ref[:, columns].astype(jnp.float32) for ref in refs]
    while len(parts) > 1:
        parts = [sum(parts[i : i + 2]) for i in range(0, len(parts), 2)]
    return parts[0]


def finish_keys(parts, cosine, sine, key_cols, width):
    rows = cosine.shape[0]

    def kernel(*refs):
        part_refs, (cos_ref, sin_ref, kv_ref, scale_ref) = refs[: len(parts)], refs[len(parts) :]
        squares = total_of(part_refs, pl.ds(2 * key_cols, HDIM))
        power = (
            squares[:, 0:1] + squares[:, 32:33] + squares[:, 64:65] + squares[:, 96:97]
        ) * (1.0 / width)
        scale = lax.rsqrt(power + eps_llm)
        scale_ref[...] = jnp.broadcast_to(scale, scale_ref.shape)
        for head in range(key_cols // HDIM):
            columns = pl.ds(head * HDIM, HDIM)
            raw = total_of(part_refs, columns) * scale
            kv_ref[:, columns] = turn(raw, cos_ref[...], sin_ref[...]).astype(jnp.bfloat16)
        columns = pl.ds(key_cols, key_cols)
        kv_ref[:, columns] = (total_of(part_refs, columns) * scale).astype(jnp.bfloat16)

    return pl.pallas_call(
        kernel,
        out_shape=(
            jax.ShapeDtypeStruct((rows, 2 * key_cols), jnp.bfloat16),
            jax.ShapeDtypeStruct((rows, HDIM), jnp.float32),
        ),
        name="finish_keys",
    )(*parts, cosine, sine)


def attend(chunks, kv, scale, cosine, sine, query_place, key_place, key_real, kv_heads):
    count, each = len(chunks), len(chunks[0])
    rows, chunk_cols = chunks[0][0].shape
    tokens = kv.shape[0]
    chunk_heads = chunk_cols // HDIM
    group = count * chunk_heads // kv_heads
    step = 2 if chunk_heads % 2 == 0 and tokens <= 2048 else 1
    factor = HDIM**-0.5

    def kernel(*refs):
        part_refs = refs[: count * each]
        scale_ref, cos_ref, sin_ref, at_ref, place_ref, real_ref, kv_ref, out_ref = refs[count * each :]
        at, place = at_ref[...], place_ref[...]
        seen = (place <= at) & ((real_ref[...] > 0) | (place == at))
        bias = jnp.where(seen, 0.0, masked_score)
        bias = jnp.concatenate([bias] * step, axis=0)
        for first in range(0, count * chunk_heads, step):
            refs_here = part_refs[first // chunk_heads * each : (first // chunk_heads + 1) * each]
            kv_head = first // group
            queries = []
            for head in range(first % chunk_heads, first % chunk_heads + step):
                raw = total_of(refs_here, pl.ds(head * HDIM, HDIM)) * scale_ref[...]
                queries.append(turn(raw, cos_ref[...], sin_ref[...]).astype(jnp.bfloat16))
            scores = lax.dot_general(
                jnp.concatenate(queries, axis=0),
                kv_ref[:, pl.ds(kv_head * HDIM, HDIM)],
                (((1,), (1,)), ((), ())),
                preferred_element_type=jnp.float32,
            )
            scores = scores * factor + bias
            top = jnp.max(scores, axis=-1, keepdims=True)
            weights = jnp.exp(scores - top)
            total = jnp.sum(weights, axis=-1, keepdims=True)
            summed = jnp.dot(
                weights.astype(jnp.bfloat16),
                kv_ref[:, pl.ds((kv_heads + kv_head) * HDIM, HDIM)],
                preferred_element_type=jnp.float32,
            )
            result = (summed / total).astype(jnp.bfloat16)
            for i in range(step):
                out_ref[:, pl.ds((first + i) * HDIM, HDIM)] = result[i * rows : (i + 1) * rows]

    flat = [part for chunk in chunks for part in chunk]
    return pl.pallas_call(
        kernel,
        out_shape=jax.ShapeDtypeStruct((rows, count * chunk_cols), jnp.bfloat16),
        compiler_params=pltpu.CompilerParams(vmem_limit_bytes=(16 << 20) * max(1, tokens // 2048)),
        name="attend",
    )(*flat, scale, cosine, sine, query_place, key_place, key_real, kv)


def project(near, frames, gain, w_qkv):
    rows, width = frames.shape
    both = near.shape[0] + rows
    wide = w_qkv.shape[1]

    def kernel(near_ref, frames_ref, gain_ref, weight_ref, out_ref):
        held = jnp.concatenate([near_ref[...], frames_ref[...]], axis=0).astype(jnp.float32)
        normed = layer_norm(held, gain_ref[...]).astype(jnp.bfloat16)
        for start in range(0, wide, width):
            columns = pl.ds(start, width)
            out_ref[:, columns] = jnp.dot(
                normed, weight_ref[:, columns], preferred_element_type=jnp.float32
            ).astype(jnp.bfloat16)

    return pl.pallas_call(
        kernel,
        out_shape=jax.ShapeDtypeStruct((both, wide), jnp.bfloat16),
        compiler_params=pltpu.CompilerParams(vmem_limit_bytes=16 << 20),
        cost_estimate=pl.CostEstimate(
            flops=2 * both * width * wide, bytes_accessed=2 * width * wide, transcendentals=0
        ),
        name="project",
    )(near, frames, gain, w_qkv)


def staged(*arrays):
    count = len(arrays)

    def kernel(*refs):
        sems = refs[-1]
        copies = [
            pltpu.make_async_copy(refs[i], refs[count + i], sems.at[i]) for i in range(count)
        ]
        for copy in copies:
            copy.start()
        for copy in copies:
            copy.wait()

    return pl.pallas_call(
        kernel,
        in_specs=[pl.BlockSpec(memory_space=pltpu.HBM)] * count,
        out_specs=(pl.BlockSpec(memory_space=pltpu.VMEM),) * count,
        out_shape=tuple(jax.ShapeDtypeStruct(array.shape, array.dtype) for array in arrays),
        scratch_shapes=[pltpu.SemaphoreType.DMA((count,))],
        compiler_params=pltpu.CompilerParams(vmem_limit_bytes=12 << 20),
        name="staged",
    )(*arrays)


def gate_frames(
    frames, proj, key_row, query_col, w_attn_out, norm_conv, w_point_in, tail_rows
):
    frame_rows, width = frames.shape
    key_rows = proj.shape[0]
    head_size = width // CH
    lanes = 2 * head_size

    def kernel(
        frames_ref, proj_ref, key_row_ref, query_col_ref, gain_ref, attn_hbm, in_hbm,
        mid_ref, glu_ref, tail_ref, attn_w, in_w, context_ref, sems,
    ):
        copies = [
            pltpu.make_async_copy(attn_hbm, attn_w, sems.at[0]),
            pltpu.make_async_copy(in_hbm, in_w, sems.at[1]),
        ]
        for copy in copies:
            copy.start()
        key_at, key_id, key_live = key_row_ref[0:1], key_row_ref[1:2], key_row_ref[2:3]
        at, ids, live = query_col_ref[:, 0:1], query_col_ref[:, 1:2], query_col_ref[:, 2:3]
        seen = (key_at <= at) & (key_id >= ids - 2) & ((key_live > 0) | (key_at == at))
        bias = jnp.where(seen, 0.0, masked_score)
        bias = jnp.concatenate([bias, bias], axis=0)
        left = lax.broadcasted_iota(jnp.int32, (frame_rows, lanes), 1) < head_size
        for pair in range(width // lanes):

            def both_rows(offset):
                columns = pl.ds(offset + pair * lanes, lanes)
                return proj_ref[:, columns]

            query = proj_ref[key_rows - frame_rows :, pl.ds(pair * lanes, lanes)]
            none = jnp.zeros_like(query)
            query = jnp.concatenate(
                [jnp.where(left, query, none), jnp.where(left, none, query)], axis=0
            )
            scores = lax.dot_general(
                query, both_rows(width), (((1,), (1,)), ((), ())), preferred_element_type=jnp.float32
            )
            scores = scores * head_size**-0.5 + bias
            top = jnp.max(scores, axis=-1, keepdims=True)
            weights = jnp.exp(scores - top)
            total = jnp.sum(weights, axis=-1, keepdims=True)
            summed = jnp.dot(
                weights.astype(jnp.bfloat16), both_rows(2 * width), preferred_element_type=jnp.float32
            )
            context = summed / total
            context_ref[:, pl.ds(pair * lanes, lanes)] = jnp.where(
                left, context[:frame_rows], context[frame_rows:]
            ).astype(jnp.bfloat16)
        copies[0].wait()
        mid = frames_ref[...].astype(jnp.float32) + jnp.dot(
            context_ref[...], attn_w[...], preferred_element_type=jnp.float32
        )
        mid_ref[...] = mid
        conv_in = layer_norm(mid, gain_ref[...]).astype(jnp.bfloat16)
        copies[1].wait()
        part = 256
        for start in range(0, width, part):
            value = jnp.dot(
                conv_in, in_w[:, pl.ds(start, part)], preferred_element_type=jnp.float32
            )
            gate = jnp.dot(
                conv_in, in_w[:, pl.ds(width + start, part)], preferred_element_type=jnp.float32
            )
            glu = jnp.where(live > 0, value * jax.nn.sigmoid(gate), 0.0).astype(jnp.bfloat16)
            glu_ref[:, pl.ds(start, part)] = glu
            tail_ref[:, pl.ds(start, part)] = glu[frame_rows - tail_rows :]

    plain = pl.BlockSpec(memory_space=pltpu.VMEM)
    apart = pl.BlockSpec(memory_space=pltpu.HBM)
    return pl.pallas_call(
        kernel,
        in_specs=[plain] * 5 + [apart] * 2,
        out_specs=(plain, plain, plain),
        out_shape=(
            jax.ShapeDtypeStruct((frame_rows, width), jnp.float32),
            jax.ShapeDtypeStruct((frame_rows, width), jnp.bfloat16),
            jax.ShapeDtypeStruct((tail_rows, width), jnp.bfloat16),
        ),
        scratch_shapes=[
            pltpu.VMEM(w_attn_out.shape, jnp.bfloat16),
            pltpu.VMEM(w_point_in.shape, jnp.bfloat16),
            pltpu.VMEM((frame_rows, width), jnp.bfloat16),
            pltpu.SemaphoreType.DMA((2,)),
        ],
        compiler_params=pltpu.CompilerParams(vmem_limit_bytes=16 << 20),
        cost_estimate=pl.CostEstimate(
            flops=2 * frame_rows * width * 3 * width,
            bytes_accessed=6 * width * width,
            transcendentals=CH * frame_rows * key_rows,
        ),
        name="gate_frames",
    )(
        frames, proj, key_row, query_col, norm_conv[None, :], w_attn_out, w_point_in
    )


def convolve_late(glu, depth_weights, extra):
    frame_rows, width = glu.shape
    taps = depth_weights.shape[0]
    late = frame_rows - extra

    def kernel(glu_ref, depth_ref, out_ref, held_ref):
        held_ref[...] = glu_ref[...].astype(jnp.float32)
        for start in range(0, width, 128):
            columns = pl.ds(start, 128)
            depth = jnp.zeros((late, 128), jnp.float32)
            for tap in range(taps):
                depth = depth + depth_ref[tap : tap + 1, columns] * held_ref[
                    pl.ds(extra - tap, late), columns
                ]
            out_ref[:, columns] = jax.nn.silu(depth).astype(jnp.bfloat16)

    return pl.pallas_call(
        kernel,
        out_shape=jax.ShapeDtypeStruct((late, width), jnp.bfloat16),
        scratch_shapes=[pltpu.VMEM((frame_rows, width), jnp.float32)],
        compiler_params=pltpu.CompilerParams(vmem_limit_bytes=8 << 20),
        cost_estimate=pl.CostEstimate(
            flops=2 * taps * late * width, bytes_accessed=4 * late * width, transcendentals=0
        ),
        name="convolve_late",
    )(glu, depth_weights)


def finish_frames(mid, glu, active, rim, real_col, depth_weights, w_point_out):
    frame_rows, width = mid.shape
    extra = rim.shape[0]
    pooled_rows = frame_rows // 4
    taps = depth_weights.shape[0]

    def kernel(
        mid_ref, glu_ref, late_ref, rim_ref, real_ref, depth_ref, out_ref, conf_ref, pooled_ref,
        held_ref, active_ref,
    ):
        held_ref[:extra] = rim_ref[...].astype(jnp.float32)
        held_ref[extra:] = glu_ref[:extra].astype(jnp.float32)
        active_ref[extra:] = late_ref[...]
        for start in range(0, width, 128):
            columns = pl.ds(start, 128)
            depth = jnp.zeros((extra, 128), jnp.float32)
            for tap in range(taps):
                depth = depth + depth_ref[tap : tap + 1, columns] * held_ref[
                    pl.ds(extra - tap, extra), columns
                ]
            active_ref[:extra, columns] = jax.nn.silu(depth).astype(jnp.bfloat16)
        final = mid_ref[...] + jnp.dot(
            active_ref[...], out_ref[...], preferred_element_type=jnp.float32
        )
        conf = jnp.where(real_ref[...] > 0, final, 0.0).astype(jnp.bfloat16)
        conf_ref[...] = conf
        row = lax.broadcasted_iota(jnp.int32, (pooled_rows, frame_rows), 0)
        column = lax.broadcasted_iota(jnp.int32, (pooled_rows, frame_rows), 1)
        mean = jnp.where(column // 4 == row, 0.25, 0.0).astype(jnp.bfloat16)
        pooled_ref[...] = jnp.dot(mean, conf, preferred_element_type=jnp.float32).astype(
            jnp.bfloat16
        )

    return pl.pallas_call(
        kernel,
        out_shape=(
            jax.ShapeDtypeStruct((frame_rows, width), jnp.bfloat16),
            jax.ShapeDtypeStruct((pooled_rows, width), jnp.bfloat16),
        ),
        scratch_shapes=[
            pltpu.VMEM((2 * extra, width), jnp.float32),
            pltpu.VMEM((frame_rows, width), jnp.bfloat16),
        ],
        compiler_params=pltpu.CompilerParams(vmem_limit_bytes=8 << 20),
        cost_estimate=pl.CostEstimate(
            flops=2 * frame_rows * width * width, bytes_accessed=2 * width * width, transcendentals=0
        ),
        name="finish_frames",
    )(mid, glu, active, rim, real_col, depth_weights, w_point_out)


def conformer(
    frames, near, first, block_ids, valid_counts, shard_frames, norm_attn, w_qkv,
    w_attn_out, norm_conv, w_point_in, depth_weights, w_point_out,
):
    before = near.shape[0]
    key_rows = before + frames.shape[0]
    key_index = first - before + jnp.arange(key_rows, dtype=jnp.int32)
    key_place, key_count = shard_count(key_index, valid_counts, shard_frames)
    key_real = (key_place < key_count) & (key_index >= 0)
    padded_ids = jnp.concatenate([jnp.full((before,), -100, jnp.int32), block_ids])
    key_ids = lax.dynamic_slice_in_dim(padded_ids, first, key_rows, 0)
    key_row = jnp.stack([key_index, key_ids, key_real.astype(jnp.int32)])
    query_col = jnp.transpose(key_row[:, before:])
    w_qkv, key_row, query_col, depth_weights = lax.optimization_barrier(
        (w_qkv, key_row, query_col, depth_weights)
    )
    held_frames, held_gain, held_weight = staged(frames, norm_attn[None, :], w_qkv)
    proj = project(near, held_frames, held_gain, held_weight)
    mid, glu, tail = gate_frames(
        frames, proj, key_row, query_col, w_attn_out, norm_conv, w_point_in, 32
    )
    rim = shifted(tail, ("tm", "mp"), 1)
    active = convolve_late(glu, depth_weights, 32)
    return finish_frames(mid, glu, active, rim, query_col[:, 2:3], depth_weights, w_point_out)


def line_pieces(value, beside):
    mp_count, place = lax.axis_size("mp"), lax.axis_index("mp")
    if mp_count != 4:
        pieces = [value] + [rotated(value, by) for by in range(1, mp_count)]
        return [jnp.stack(pieces)], lambda source: (place - source) % mp_count, beside
    below = lax.ppermute(value, "mp", [(0, 1), (1, 2), (2, 3)])
    above = lax.ppermute(value, "mp", [(1, 0), (2, 1), (3, 2)])
    half = value.shape[0] // 2
    own, below, above, beside = lax.optimization_barrier(
        ((value[:half], value[half:]), below, above, beside)
    )
    chunks, waiting = [], (own, below, above)
    for start in (0, half):
        own, below, above = waiting
        mine, lower, upper = own[start // half], below[start : start + half], above[start : start + half]
        far = lax.ppermute(mine, "mp", [(0, 3), (3, 0)])
        lower_2 = lax.ppermute(lower, "mp", [(1, 2), (2, 3)])
        upper_2 = lax.ppermute(upper, "mp", [(2, 1), (1, 0)])
        if start == 0:
            far, lower_2, upper_2, waiting = lax.optimization_barrier(
                (far, lower_2, upper_2, waiting)
            )
        chunks.append(jnp.stack([far, lower_2, lower, mine, upper, upper_2]))
    return chunks, lambda source: (source - place + 3) % 6, beside


def chip_adapter_columns(stacked, row_of):
    tm_count = lax.axis_size("tm")
    time_place = lax.axis_index("tm")
    kept = []
    for other in range(0, tm_count, 2):
        wanted = (time_place ^ other) // 2
        piece = lax.dynamic_index_in_dim(stacked, row_of(wanted), 0, keepdims=False)
        kept.append(swapped(piece, other) if other else piece)
    return kept


def adapt(pooled, near, gain, w_key, w_value):
    tm_count, time_place = lax.axis_size("tm"), lax.axis_index("tm")
    part, cols = near[0][0].shape
    half = cols // 2
    tokens, depth = pooled.shape
    flat = [array for chunk in near for array in chunk]
    place_word = time_place.reshape(1).astype(jnp.int32)
    plain = pl.BlockSpec(memory_space=pltpu.VMEM)
    scalar = pl.BlockSpec(memory_space=pltpu.SMEM)

    def halves(place_ref, *refs):
        for away, out_ref in enumerate(refs[-2:]):
            columns = pl.ds(pl.multiple_of((place_ref[0] + away) % 2 * half, 128), half)
            for i, ref in enumerate(refs[:-2]):
                out_ref[i * part : (i + 1) * part, :] = ref[:, columns]

    mine, given = pl.pallas_call(
        halves,
        in_specs=[scalar] + [plain] * len(flat),
        out_specs=(plain, plain),
        out_shape=(jax.ShapeDtypeStruct((len(flat) * part, half), jnp.bfloat16),) * 2,
        compiler_params=pltpu.CompilerParams(vmem_limit_bytes=4 << 20),
        name="halves",
    )(place_word, *flat)
    taken = swapped(given, 1)
    step, key_cols = min(256, tokens), w_key.shape[1]

    def kernel(
        place_ref, mine_ref, taken_ref, pooled_ref, gain_ref, key_ref, value_ref, out_ref, kv_ref,
        weight_ref,
    ):
        place = place_ref[0]
        for i in range(len(flat)):
            chunk, other = i // (tm_count // 2), 2 * (i % (tm_count // 2))
            for shift, ref in enumerate((mine_ref, taken_ref)):
                source = place ^ (other + shift)
                row = pl.multiple_of(source * (part * len(near)) + chunk * part, part)
                weight_ref[pl.ds(row, part), :] = ref[i * part : (i + 1) * part]
        lane = lax.broadcasted_iota(jnp.int32, (step, HDIM), 1) // 32 - 2 * (place % 2)
        for start in range(0, tokens, step):
            rows = pl.ds(start, step)
            adapted = jnp.dot(
                pooled_ref[rows, :], weight_ref[...], preferred_element_type=jnp.float32
            )
            scaled = (adapted * gain_ref[...]).astype(jnp.bfloat16)
            out_ref[rows, :] = scaled
            for i, ref in enumerate((key_ref, value_ref)):
                kv_ref[rows, pl.ds(i * key_cols, key_cols)] = jnp.dot(
                    scaled, ref[...], preferred_element_type=jnp.float32
                ).astype(jnp.bfloat16)
            squares = jnp.sum(adapted * adapted, axis=-1, keepdims=True)
            high = squares.astype(jnp.bfloat16).astype(jnp.float32)
            words = jnp.where(lane == 0, high, jnp.where(lane == 1, squares - high, 0.0))
            kv_ref[rows, pl.ds(2 * key_cols, HDIM)] = words.astype(jnp.bfloat16)

    return pl.pallas_call(
        kernel,
        in_specs=[scalar] + [plain] * 6,
        out_specs=(plain, plain),
        out_shape=(
            jax.ShapeDtypeStruct((tokens, half), jnp.bfloat16),
            jax.ShapeDtypeStruct((tokens, 2 * key_cols + HDIM), jnp.bfloat16),
        ),
        scratch_shapes=[pltpu.VMEM((depth, half), jnp.bfloat16)],
        compiler_params=pltpu.CompilerParams(vmem_limit_bytes=18 << 20),
        name="adapt",
    )(place_word, mine, taken, pooled, gain[None, :], w_key, w_value)


def spread_even(value):
    tm_count = lax.axis_size("tm")
    blocks = [value] + [swapped(value, other) for other in range(2, tm_count, 2)]
    return jnp.concatenate(blocks, axis=0)


def spread(even):
    return jnp.concatenate([even, swapped(even, 1)], axis=0)


def both_sum(one, other):
    return (one.astype(jnp.float32) + other.astype(jnp.float32)).astype(jnp.bfloat16)


def direct_parts(value):
    tm_count = lax.axis_size("tm")
    half = value.shape[0] // 2
    rows = value.shape[0] // tm_count
    chip = both_sum(value[:half], swapped(value[half:], 1))
    return [chip[:rows]] + [
        swapped(chip[i * rows : (i + 1) * rows], 2 * i) for i in range(1, tm_count // 2)
    ]


def chip_sum(left, right, weight):
    def product(rows):
        return jnp.dot(rows, weight, preferred_element_type=jnp.float32)

    other = swapped(product(right).astype(jnp.bfloat16), 1)
    return (product(left) + other.astype(jnp.float32)).astype(jnp.bfloat16)


def halved(held, bit, axes):
    axis = axes.index(bit)
    keep = lax.index_in_dim(held, 0, axis, keepdims=False)
    given = lax.index_in_dim(held, 1, axis, keepdims=False)
    return keep, swapped(given, 2 << bit), axes[:axis] + axes[axis + 1 :]


def on_device(
    frames,
    block_ids,
    valid_counts,
    norm_attn,
    w_qkv,
    w_attn_out,
    norm_conv,
    w_point_in,
    w_depth,
    w_point_out,
    w_adapter,
    llm_gain,
    w_query,
    w_key,
    w_value,
):
    tm_count, mp_count = lax.axis_size("tm"), lax.axis_size("mp")
    time_place, model_place = lax.axis_index("tm"), lax.axis_index("mp")
    frame_rows, width = frames.shape
    shard_frames = frame_rows * mp_count
    first = (time_place * mp_count + model_place) * frame_rows
    near = shifted(frames, ("tm", "mp"), 1)
    depth_weights = w_depth.astype(jnp.float32)
    w_adapter, near = lax.optimization_barrier((w_adapter, near))
    conf_out, pooled = conformer(
        frames, near, first, block_ids, valid_counts, shard_frames, norm_attn, w_qkv,
        w_attn_out, norm_conv, w_point_in, depth_weights, w_point_out,
    )
    stacked, row_of, pooled = line_pieces(w_adapter, pooled)
    pooled, late_place, late_counts = lax.optimization_barrier((pooled, time_place, valid_counts))
    piece = pooled.shape[0]
    shard_tokens = piece * mp_count
    cycle = [rotated(pooled, by) for by in range(mp_count - 1, 0, -1)] + [pooled]
    shard_pooled = lax.dynamic_slice_in_dim(
        jnp.concatenate(cycle + cycle, axis=0), (mp_count - 1 - model_place) * piece, shard_tokens, 0
    )
    even_pooled, stacked[0] = lax.optimization_barrier((spread_even(shard_pooled), stacked[0]))
    all_pooled, near_columns = lax.optimization_barrier(
        (
            spread(even_pooled),
            [chip_adapter_columns(chunk, row_of) for chunk in stacked],
        )
    )
    tokens = all_pooled.shape[0]
    block = w_adapter.shape[1] * mp_count // tm_count
    gain = lax.dynamic_slice_in_dim(llm_gain, time_place * block, block, 0)
    scaled, kv_raw = adapt(all_pooled, near_columns, gain, w_key, w_value)
    key_cols, half_cols = w_key.shape[1], w_query.shape[1] // 2
    kv_parts = direct_parts(kv_raw)
    bits = list(range(tm_count.bit_length() - 2))
    left, right = scaled[: tokens // 2], scaled[tokens // 2 :]
    sums = [
        chip_sum(left, right, w_query[:, :half_cols]),
        chip_sum(left, right, w_query[:, half_cols:]),
    ]
    kv_parts, _ = lax.optimization_barrier((kv_parts, sums))
    query_chunks, rest = [], [bits, bits[::-1]]
    for held, turns in zip(sums, rest):
        held = held.reshape((2,) * len(bits) + (shard_tokens, half_cols))
        keep, taken, left_axes = halved(held, turns[0], bits[::-1])
        for turn_bit in turns[1:]:
            keep, taken, left_axes = halved(both_sum(keep, taken), turn_bit, left_axes)
        query_chunks.append((keep, taken))
    order = list(range(0, tm_count, 2)) + list(range(1, tm_count, 2))
    within = jnp.arange(shard_tokens, dtype=jnp.int32)
    own_place = late_place * shard_tokens + within
    cosine, sine = rotary_tables(own_place, HDIM)
    kv, scale = finish_keys(kv_parts, cosine, sine, key_cols, block * tm_count)
    all_kv = spread(spread_even(kv))
    key_place = jnp.concatenate([(late_place ^ other) * shard_tokens + within for other in order])
    place_in, counts = shard_count(key_place, late_counts, shard_tokens)
    key_real = (place_in * 4 < counts).astype(jnp.int32)
    attended = attend(
        query_chunks, all_kv, scale, cosine, sine, own_place[:, None], key_place[None, :],
        key_real[None, :], key_cols // HDIM,
    )
    return (conf_out, attended)


def solution(mesh):
    placed = (
        P(("tm", "mp"), None),
        P(),
        P(),
        P(),
        P(),
        P(),
        P(),
        P(),
        P(),
        P(),
        P("tm", "mp"),
        P(),
        P("tm", "mp"),
        P("tm", "mp"),
        P("tm", "mp"),
    )
    return jax.shard_map(
        on_device,
        mesh=mesh,
        in_specs=placed,
        out_specs=(P(("tm", "mp"), None), P("tm", "mp")),
        check_vma=False,
    )
```

```python
import jax
import jax.numpy as jnp
from jax import lax
from jax.experimental import pallas as pl
from jax.experimental.pallas import tpu as pltpu
from jax.sharding import PartitionSpec as P

CH = 16
HDIM = 128
SPAN = 40


eps_conf = 1e-05
eps_llm = 1e-06
rope_base = 1000000.0
masked_score = -1e30


def shifted(value, axis, by):
    length = lax.axis_size(axis)
    return lax.ppermute(value, axis, [(i, i + by) for i in range(length - by)])


def swapped(value, bits):
    length = lax.axis_size("tm")
    return lax.ppermute(value, "tm", [(i, i ^ bits) for i in range(length)])


def rotated(value, by):
    length = lax.axis_size("mp")
    return lax.ppermute(value, "mp", [(i, (i + by) % length) for i in range(length)])


def shard_count(index, valid_counts, shard_len):
    shard = index // shard_len
    table = jnp.arange(valid_counts.shape[0], dtype=jnp.int32)
    hit = shard[:, None] == table[None, :]
    count = jnp.sum(jnp.where(hit, valid_counts[None, :], 0), axis=1)
    return (index - shard * shard_len, count)


def layer_norm(field, gain):
    center = field - jnp.mean(field, axis=-1, keepdims=True)
    spread = jnp.mean(center * center, axis=-1, keepdims=True)
    return center * lax.rsqrt(spread + eps_conf) * gain


def rotary_tables(positions, size):
    half = size // 2
    freq = rope_base ** (-(jnp.arange(half, dtype=jnp.float32) * 2.0) / size)
    angle = positions.astype(jnp.float32)[:, None] * freq[None, :]
    cosine = jnp.concatenate([jnp.cos(angle), jnp.cos(angle)], axis=-1)
    sine = jnp.concatenate([-jnp.sin(angle), jnp.sin(angle)], axis=-1)
    return cosine, sine


def turn(field, cosine, sine):
    return field * cosine + pltpu.roll(field, HDIM // 2, 1) * sine


def total_of(refs, columns):
    parts = [ref[:, columns].astype(jnp.float32) for ref in refs]
    while len(parts) > 1:
        parts = [sum(parts[i : i + 2]) for i in range(0, len(parts), 2)]
    return parts[0]


def finish_keys(parts, cosine, sine, key_cols, width):
    rows = cosine.shape[0]

    def kernel(*refs):
        part_refs, (cos_ref, sin_ref, kv_ref, scale_ref) = refs[: len(parts)], refs[len(parts) :]
        squares = total_of(part_refs, pl.ds(2 * key_cols, HDIM))
        power = (
            squares[:, 0:1] + squares[:, 32:33] + squares[:, 64:65] + squares[:, 96:97]
        ) * (1.0 / width)
        scale = lax.rsqrt(power + eps_llm)
        scale_ref[...] = jnp.broadcast_to(scale, scale_ref.shape)
        for head in range(key_cols // HDIM):
            columns = pl.ds(head * HDIM, HDIM)
            raw = total_of(part_refs, columns) * scale
            kv_ref[:, columns] = turn(raw, cos_ref[...], sin_ref[...]).astype(jnp.bfloat16)
        columns = pl.ds(key_cols, key_cols)
        kv_ref[:, columns] = (total_of(part_refs, columns) * scale).astype(jnp.bfloat16)

    return pl.pallas_call(
        kernel,
        out_shape=(
            jax.ShapeDtypeStruct((rows, 2 * key_cols), jnp.bfloat16),
            jax.ShapeDtypeStruct((rows, HDIM), jnp.float32),
        ),
        name="finish_keys",
    )(*parts, cosine, sine)


def attend(chunks, kv, scale, cosine, sine, query_place, key_place, key_real, kv_heads):
    count, each = len(chunks), len(chunks[0])
    rows, chunk_cols = chunks[0][0].shape
    tokens = kv.shape[0]
    chunk_heads = chunk_cols // HDIM
    group = count * chunk_heads // kv_heads
    step = 4 if chunk_heads % 4 == 0 and tokens <= 1024 else 1
    factor = HDIM**-0.5

    def kernel(*refs):
        part_refs = refs[: count * each]
        scale_ref, cos_ref, sin_ref, at_ref, place_ref, real_ref, kv_ref, out_ref = refs[count * each :]
        at, place = at_ref[...], place_ref[...]
        seen = (place <= at) & ((real_ref[...] > 0) | (place == at))
        bias = jnp.where(seen, 0.0, masked_score)
        bias = jnp.concatenate([bias] * step, axis=0)
        for first in range(0, count * chunk_heads, step):
            refs_here = part_refs[first // chunk_heads * each : (first // chunk_heads + 1) * each]
            kv_head = first // group
            queries = []
            for head in range(first % chunk_heads, first % chunk_heads + step):
                raw = total_of(refs_here, pl.ds(head * HDIM, HDIM)) * scale_ref[...]
                queries.append(turn(raw, cos_ref[...], sin_ref[...]).astype(jnp.bfloat16))
            scores = lax.dot_general(
                jnp.concatenate(queries, axis=0),
                kv_ref[:, pl.ds(kv_head * HDIM, HDIM)],
                (((1,), (1,)), ((), ())),
                preferred_element_type=jnp.float32,
            )
            scores = scores * factor + bias
            top = jnp.max(scores, axis=-1, keepdims=True)
            weights = jnp.exp(scores - top)
            total = jnp.sum(weights, axis=-1, keepdims=True)
            summed = jnp.dot(
                weights.astype(jnp.bfloat16),
                kv_ref[:, pl.ds((kv_heads + kv_head) * HDIM, HDIM)],
                preferred_element_type=jnp.float32,
            )
            result = (summed / total).astype(jnp.bfloat16)
            for i in range(step):
                out_ref[:, pl.ds((first + i) * HDIM, HDIM)] = result[i * rows : (i + 1) * rows]

    flat = [part for chunk in chunks for part in chunk]
    return pl.pallas_call(
        kernel,
        out_shape=jax.ShapeDtypeStruct((rows, count * chunk_cols), jnp.bfloat16),
        compiler_params=pltpu.CompilerParams(vmem_limit_bytes=(16 << 20) * max(1, tokens // 2048)),
        name="attend",
    )(*flat, scale, cosine, sine, query_place, key_place, key_real, kv)


def project(near, frames, gain, w_qkv):
    rows, width = frames.shape
    both = near.shape[0] + rows
    wide = w_qkv.shape[1]

    def kernel(near_ref, frames_ref, gain_ref, weight_ref, out_ref):
        held = jnp.concatenate([near_ref[...], frames_ref[...]], axis=0).astype(jnp.float32)
        normed = layer_norm(held, gain_ref[...]).astype(jnp.bfloat16)
        for start in range(0, wide, width):
            columns = pl.ds(start, width)
            out_ref[:, columns] = jnp.dot(
                normed, weight_ref[:, columns], preferred_element_type=jnp.float32
            ).astype(jnp.bfloat16)

    return pl.pallas_call(
        kernel,
        out_shape=jax.ShapeDtypeStruct((both, wide), jnp.bfloat16),
        compiler_params=pltpu.CompilerParams(vmem_limit_bytes=16 << 20),
        cost_estimate=pl.CostEstimate(
            flops=2 * both * width * wide, bytes_accessed=2 * width * wide, transcendentals=0
        ),
        name="project",
    )(near, frames, gain, w_qkv)


def staged(*arrays):
    count = len(arrays)

    def kernel(*refs):
        sems = refs[-1]
        copies = [
            pltpu.make_async_copy(refs[i], refs[count + i], sems.at[i]) for i in range(count)
        ]
        for copy in copies:
            copy.start()
        for copy in copies:
            copy.wait()

    return pl.pallas_call(
        kernel,
        in_specs=[pl.BlockSpec(memory_space=pltpu.HBM)] * count,
        out_specs=(pl.BlockSpec(memory_space=pltpu.VMEM),) * count,
        out_shape=tuple(jax.ShapeDtypeStruct(array.shape, array.dtype) for array in arrays),
        scratch_shapes=[pltpu.SemaphoreType.DMA((count,))],
        compiler_params=pltpu.CompilerParams(vmem_limit_bytes=12 << 20),
        name="staged",
    )(*arrays)


def gate_frames(
    frames, proj, key_row, query_col, w_attn_out, norm_conv, w_point_in, tail_rows
):
    frame_rows, width = frames.shape
    key_rows = proj.shape[0]
    head_size = width // CH
    lanes = 2 * head_size

    def kernel(
        frames_ref, proj_ref, key_row_ref, query_col_ref, gain_ref, attn_hbm, in_hbm,
        mid_ref, glu_ref, tail_ref, attn_w, in_w, context_ref, sems,
    ):
        copies = [
            pltpu.make_async_copy(attn_hbm, attn_w, sems.at[0]),
            pltpu.make_async_copy(in_hbm, in_w, sems.at[1]),
        ]
        for copy in copies:
            copy.start()
        key_at, key_id, key_live = key_row_ref[0:1], key_row_ref[1:2], key_row_ref[2:3]
        at, ids, live = query_col_ref[:, 0:1], query_col_ref[:, 1:2], query_col_ref[:, 2:3]
        seen = (key_at <= at) & (key_id >= ids - 2) & ((key_live > 0) | (key_at == at))
        bias = jnp.where(seen, 0.0, masked_score)
        bias = jnp.concatenate([bias, bias], axis=0)
        left = lax.broadcasted_iota(jnp.int32, (frame_rows, lanes), 1) < head_size
        for pair in range(width // lanes):

            def both_rows(offset):
                columns = pl.ds(offset + pair * lanes, lanes)
                return proj_ref[:, columns]

            query = proj_ref[key_rows - frame_rows :, pl.ds(pair * lanes, lanes)]
            none = jnp.zeros_like(query)
            query = jnp.concatenate(
                [jnp.where(left, query, none), jnp.where(left, none, query)], axis=0
            )
            scores = lax.dot_general(
                query, both_rows(width), (((1,), (1,)), ((), ())), preferred_element_type=jnp.float32
            )
            scores = scores * head_size**-0.5 + bias
            top = jnp.max(scores, axis=-1, keepdims=True)
            weights = jnp.exp(scores - top)
            total = jnp.sum(weights, axis=-1, keepdims=True)
            summed = jnp.dot(
                weights.astype(jnp.bfloat16), both_rows(2 * width), preferred_element_type=jnp.float32
            )
            context = summed / total
            context_ref[:, pl.ds(pair * lanes, lanes)] = jnp.where(
                left, context[:frame_rows], context[frame_rows:]
            ).astype(jnp.bfloat16)
        copies[0].wait()
        mid = frames_ref[...].astype(jnp.float32) + jnp.dot(
            context_ref[...], attn_w[...], preferred_element_type=jnp.float32
        )
        mid_ref[...] = mid
        conv_in = layer_norm(mid, gain_ref[...]).astype(jnp.bfloat16)
        copies[1].wait()
        part = 256
        for start in range(0, width, part):
            value = jnp.dot(
                conv_in, in_w[:, pl.ds(start, part)], preferred_element_type=jnp.float32
            )
            gate = jnp.dot(
                conv_in, in_w[:, pl.ds(width + start, part)], preferred_element_type=jnp.float32
            )
            glu = jnp.where(live > 0, value * jax.nn.sigmoid(gate), 0.0).astype(jnp.bfloat16)
            glu_ref[:, pl.ds(start, part)] = glu
            tail_ref[:, pl.ds(start, part)] = glu[frame_rows - tail_rows :]

    plain = pl.BlockSpec(memory_space=pltpu.VMEM)
    apart = pl.BlockSpec(memory_space=pltpu.HBM)
    return pl.pallas_call(
        kernel,
        in_specs=[plain] * 5 + [apart] * 2,
        out_specs=(plain, plain, plain),
        out_shape=(
            jax.ShapeDtypeStruct((frame_rows, width), jnp.float32),
            jax.ShapeDtypeStruct((frame_rows, width), jnp.bfloat16),
            jax.ShapeDtypeStruct((tail_rows, width), jnp.bfloat16),
        ),
        scratch_shapes=[
            pltpu.VMEM(w_attn_out.shape, jnp.bfloat16),
            pltpu.VMEM(w_point_in.shape, jnp.bfloat16),
            pltpu.VMEM((frame_rows, width), jnp.bfloat16),
            pltpu.SemaphoreType.DMA((2,)),
        ],
        compiler_params=pltpu.CompilerParams(vmem_limit_bytes=16 << 20),
        cost_estimate=pl.CostEstimate(
            flops=2 * frame_rows * width * 3 * width,
            bytes_accessed=6 * width * width,
            transcendentals=CH * frame_rows * key_rows,
        ),
        name="gate_frames",
    )(
        frames, proj, key_row, query_col, norm_conv[None, :], w_attn_out, w_point_in
    )


def convolve_late(glu, depth_weights, extra):
    frame_rows, width = glu.shape
    taps = depth_weights.shape[0]
    late = frame_rows - extra

    def kernel(glu_ref, depth_ref, out_ref, held_ref):
        held_ref[...] = glu_ref[...].astype(jnp.float32)
        for start in range(0, width, 128):
            columns = pl.ds(start, 128)
            depth = jnp.zeros((late, 128), jnp.float32)
            for tap in range(taps):
                depth = depth + depth_ref[tap : tap + 1, columns] * held_ref[
                    pl.ds(extra - tap, late), columns
                ]
            out_ref[:, columns] = jax.nn.silu(depth).astype(jnp.bfloat16)

    return pl.pallas_call(
        kernel,
        out_shape=jax.ShapeDtypeStruct((late, width), jnp.bfloat16),
        scratch_shapes=[pltpu.VMEM((frame_rows, width), jnp.float32)],
        compiler_params=pltpu.CompilerParams(vmem_limit_bytes=8 << 20),
        cost_estimate=pl.CostEstimate(
            flops=2 * taps * late * width, bytes_accessed=4 * late * width, transcendentals=0
        ),
        name="convolve_late",
    )(glu, depth_weights)


def finish_frames(mid, glu, active, rim, real_col, depth_weights, w_point_out):
    frame_rows, width = mid.shape
    extra = rim.shape[0]
    pooled_rows = frame_rows // 4
    taps = depth_weights.shape[0]

    def kernel(
        mid_ref, glu_ref, late_ref, rim_ref, real_ref, depth_ref, out_ref, conf_ref, pooled_ref,
        held_ref, active_ref,
    ):
        held_ref[:extra] = rim_ref[...].astype(jnp.float32)
        held_ref[extra:] = glu_ref[:extra].astype(jnp.float32)
        active_ref[extra:] = late_ref[...]
        for start in range(0, width, 128):
            columns = pl.ds(start, 128)
            depth = jnp.zeros((extra, 128), jnp.float32)
            for tap in range(taps):
                depth = depth + depth_ref[tap : tap + 1, columns] * held_ref[
                    pl.ds(extra - tap, extra), columns
                ]
            active_ref[:extra, columns] = jax.nn.silu(depth).astype(jnp.bfloat16)
        final = mid_ref[...] + jnp.dot(
            active_ref[...], out_ref[...], preferred_element_type=jnp.float32
        )
        conf = jnp.where(real_ref[...] > 0, final, 0.0).astype(jnp.bfloat16)
        conf_ref[...] = conf
        row = lax.broadcasted_iota(jnp.int32, (pooled_rows, frame_rows), 0)
        column = lax.broadcasted_iota(jnp.int32, (pooled_rows, frame_rows), 1)
        mean = jnp.where(column // 4 == row, 0.25, 0.0).astype(jnp.bfloat16)
        pooled_ref[...] = jnp.dot(mean, conf, preferred_element_type=jnp.float32).astype(
            jnp.bfloat16
        )

    return pl.pallas_call(
        kernel,
        out_shape=(
            jax.ShapeDtypeStruct((frame_rows, width), jnp.bfloat16),
            jax.ShapeDtypeStruct((pooled_rows, width), jnp.bfloat16),
        ),
        scratch_shapes=[
            pltpu.VMEM((2 * extra, width), jnp.float32),
            pltpu.VMEM((frame_rows, width), jnp.bfloat16),
        ],
        compiler_params=pltpu.CompilerParams(vmem_limit_bytes=8 << 20),
        cost_estimate=pl.CostEstimate(
            flops=2 * frame_rows * width * width, bytes_accessed=2 * width * width, transcendentals=0
        ),
        name="finish_frames",
    )(mid, glu, active, rim, real_col, depth_weights, w_point_out)


def conformer(
    frames, near, first, block_ids, valid_counts, shard_frames, norm_attn, w_qkv,
    w_attn_out, norm_conv, w_point_in, depth_weights, w_point_out,
):
    before = near.shape[0]
    key_rows = before + frames.shape[0]
    key_index = first - before + jnp.arange(key_rows, dtype=jnp.int32)
    key_place, key_count = shard_count(key_index, valid_counts, shard_frames)
    key_real = (key_place < key_count) & (key_index >= 0)
    padded_ids = jnp.concatenate([jnp.full((before,), -100, jnp.int32), block_ids])
    key_ids = lax.dynamic_slice_in_dim(padded_ids, first, key_rows, 0)
    key_row = jnp.stack([key_index, key_ids, key_real.astype(jnp.int32)])
    query_col = jnp.transpose(key_row[:, before:])
    w_qkv, key_row, query_col, depth_weights = lax.optimization_barrier(
        (w_qkv, key_row, query_col, depth_weights)
    )
    held_frames, held_gain, held_weight = staged(frames, norm_attn[None, :], w_qkv)
    proj = project(near, held_frames, held_gain, held_weight)
    mid, glu, tail = gate_frames(
        frames, proj, key_row, query_col, w_attn_out, norm_conv, w_point_in, 32
    )
    rim = shifted(tail, ("tm", "mp"), 1)
    active = convolve_late(glu, depth_weights, 32)
    return finish_frames(mid, glu, active, rim, query_col[:, 2:3], depth_weights, w_point_out)


def line_pieces(value, beside):
    mp_count, place = lax.axis_size("mp"), lax.axis_index("mp")
    if mp_count != 4:
        pieces = [value] + [rotated(value, by) for by in range(1, mp_count)]
        return [jnp.stack(pieces)], lambda source: (place - source) % mp_count, beside
    below = lax.ppermute(value, "mp", [(0, 1), (1, 2), (2, 3)])
    above = lax.ppermute(value, "mp", [(1, 0), (2, 1), (3, 2)])
    half = value.shape[0] // 2
    own, below, above, beside = lax.optimization_barrier(
        ((value[:half], value[half:]), below, above, beside)
    )
    chunks, waiting = [], (own, below, above)
    for start in (0, half):
        own, below, above = waiting
        mine, lower, upper = own[start // half], below[start : start + half], above[start : start + half]
        far = lax.ppermute(mine, "mp", [(0, 3), (3, 0)])
        lower_2 = lax.ppermute(lower, "mp", [(1, 2), (2, 3)])
        upper_2 = lax.ppermute(upper, "mp", [(2, 1), (1, 0)])
        if start == 0:
            far, lower_2, upper_2, waiting = lax.optimization_barrier(
                (far, lower_2, upper_2, waiting)
            )
        chunks.append(jnp.stack([far, lower_2, lower, mine, upper, upper_2]))
    return chunks, lambda source: (source - place + 3) % 6, beside


def chip_adapter_columns(stacked, row_of):
    tm_count = lax.axis_size("tm")
    time_place = lax.axis_index("tm")
    kept = []
    for other in range(0, tm_count, 2):
        wanted = (time_place ^ other) // 2
        piece = lax.dynamic_index_in_dim(stacked, row_of(wanted), 0, keepdims=False)
        kept.append(swapped(piece, other) if other else piece)
    return kept


def adapt(pooled, near, gain, w_key, w_value):
    tm_count, time_place = lax.axis_size("tm"), lax.axis_index("tm")
    part, cols = near[0][0].shape
    half = cols // 2
    tokens, depth = pooled.shape
    flat = [array for chunk in near for array in chunk]
    place_word = time_place.reshape(1).astype(jnp.int32)
    plain = pl.BlockSpec(memory_space=pltpu.VMEM)
    scalar = pl.BlockSpec(memory_space=pltpu.SMEM)

    def halves(place_ref, *refs):
        for away, out_ref in enumerate(refs[-2:]):
            columns = pl.ds(pl.multiple_of((place_ref[0] + away) % 2 * half, 128), half)
            for i, ref in enumerate(refs[:-2]):
                out_ref[i * part : (i + 1) * part, :] = ref[:, columns]

    mine, given = pl.pallas_call(
        halves,
        in_specs=[scalar] + [plain] * len(flat),
        out_specs=(plain, plain),
        out_shape=(jax.ShapeDtypeStruct((len(flat) * part, half), jnp.bfloat16),) * 2,
        compiler_params=pltpu.CompilerParams(vmem_limit_bytes=4 << 20),
        name="halves",
    )(place_word, *flat)
    taken = swapped(given, 1)
    step, key_cols = min(256, tokens), w_key.shape[1]

    def kernel(
        place_ref, mine_ref, taken_ref, pooled_ref, gain_ref, key_ref, value_ref, out_ref, kv_ref,
        weight_ref,
    ):
        place = place_ref[0]
        for i in range(len(flat)):
            chunk, other = i // (tm_count // 2), 2 * (i % (tm_count // 2))
            for shift, ref in enumerate((mine_ref, taken_ref)):
                source = place ^ (other + shift)
                row = pl.multiple_of(source * (part * len(near)) + chunk * part, part)
                weight_ref[pl.ds(row, part), :] = ref[i * part : (i + 1) * part]
        lane = lax.broadcasted_iota(jnp.int32, (step, HDIM), 1) // 32 - 2 * (place % 2)
        for start in range(0, tokens, step):
            rows = pl.ds(start, step)
            adapted = jnp.dot(
                pooled_ref[rows, :], weight_ref[...], preferred_element_type=jnp.float32
            )
            scaled = (adapted * gain_ref[...]).astype(jnp.bfloat16)
            out_ref[rows, :] = scaled
            for i, ref in enumerate((key_ref, value_ref)):
                kv_ref[rows, pl.ds(i * key_cols, key_cols)] = jnp.dot(
                    scaled, ref[...], preferred_element_type=jnp.float32
                ).astype(jnp.bfloat16)
            squares = jnp.sum(adapted * adapted, axis=-1, keepdims=True)
            high = squares.astype(jnp.bfloat16).astype(jnp.float32)
            words = jnp.where(lane == 0, high, jnp.where(lane == 1, squares - high, 0.0))
            kv_ref[rows, pl.ds(2 * key_cols, HDIM)] = words.astype(jnp.bfloat16)

    return pl.pallas_call(
        kernel,
        in_specs=[scalar] + [plain] * 6,
        out_specs=(plain, plain),
        out_shape=(
            jax.ShapeDtypeStruct((tokens, half), jnp.bfloat16),
            jax.ShapeDtypeStruct((tokens, 2 * key_cols + HDIM), jnp.bfloat16),
        ),
        scratch_shapes=[pltpu.VMEM((depth, half), jnp.bfloat16)],
        compiler_params=pltpu.CompilerParams(vmem_limit_bytes=18 << 20),
        name="adapt",
    )(place_word, mine, taken, pooled, gain[None, :], w_key, w_value)


def spread_even(value):
    tm_count = lax.axis_size("tm")
    blocks = [value] + [swapped(value, other) for other in range(2, tm_count, 2)]
    return jnp.concatenate(blocks, axis=0)


def spread(even):
    return jnp.concatenate([even, swapped(even, 1)], axis=0)


def both_sum(one, other):
    return (one.astype(jnp.float32) + other.astype(jnp.float32)).astype(jnp.bfloat16)


def direct_parts(value):
    tm_count = lax.axis_size("tm")
    half = value.shape[0] // 2
    rows = value.shape[0] // tm_count
    chip = both_sum(value[:half], swapped(value[half:], 1))
    return [chip[:rows]] + [
        swapped(chip[i * rows : (i + 1) * rows], 2 * i) for i in range(1, tm_count // 2)
    ]


def chip_sum(left, right, weight):
    def product(rows):
        return jnp.dot(rows, weight, preferred_element_type=jnp.float32)

    other = swapped(product(right).astype(jnp.bfloat16), 1)
    return (product(left) + other.astype(jnp.float32)).astype(jnp.bfloat16)


def halved(held, bit, axes):
    axis = axes.index(bit)
    keep = lax.index_in_dim(held, 0, axis, keepdims=False)
    given = lax.index_in_dim(held, 1, axis, keepdims=False)
    return keep, swapped(given, 2 << bit), axes[:axis] + axes[axis + 1 :]


def on_device(
    frames,
    block_ids,
    valid_counts,
    norm_attn,
    w_qkv,
    w_attn_out,
    norm_conv,
    w_point_in,
    w_depth,
    w_point_out,
    w_adapter,
    llm_gain,
    w_query,
    w_key,
    w_value,
):
    tm_count, mp_count = lax.axis_size("tm"), lax.axis_size("mp")
    time_place, model_place = lax.axis_index("tm"), lax.axis_index("mp")
    frame_rows, width = frames.shape
    shard_frames = frame_rows * mp_count
    first = (time_place * mp_count + model_place) * frame_rows
    near = shifted(frames, ("tm", "mp"), 1)
    depth_weights = w_depth.astype(jnp.float32)
    w_adapter, near = lax.optimization_barrier((w_adapter, near))
    conf_out, pooled = conformer(
        frames, near, first, block_ids, valid_counts, shard_frames, norm_attn, w_qkv,
        w_attn_out, norm_conv, w_point_in, depth_weights, w_point_out,
    )
    stacked, row_of, pooled = line_pieces(w_adapter, pooled)
    pooled, late_place, late_counts = lax.optimization_barrier((pooled, time_place, valid_counts))
    piece = pooled.shape[0]
    shard_tokens = piece * mp_count
    cycle = [rotated(pooled, by) for by in range(mp_count - 1, 0, -1)] + [pooled]
    shard_pooled = lax.dynamic_slice_in_dim(
        jnp.concatenate(cycle + cycle, axis=0), (mp_count - 1 - model_place) * piece, shard_tokens, 0
    )
    even_pooled, stacked[0] = lax.optimization_barrier((spread_even(shard_pooled), stacked[0]))
    all_pooled, near_columns = lax.optimization_barrier(
        (
            spread(even_pooled),
            [chip_adapter_columns(chunk, row_of) for chunk in stacked],
        )
    )
    tokens = all_pooled.shape[0]
    block = w_adapter.shape[1] * mp_count // tm_count
    gain = lax.dynamic_slice_in_dim(llm_gain, time_place * block, block, 0)
    scaled, kv_raw = adapt(all_pooled, near_columns, gain, w_key, w_value)
    key_cols, half_cols = w_key.shape[1], w_query.shape[1] // 2
    kv_parts = direct_parts(kv_raw)
    bits = list(range(tm_count.bit_length() - 2))
    left, right = scaled[: tokens // 2], scaled[tokens // 2 :]
    sums = [
        chip_sum(left, right, w_query[:, :half_cols]),
        chip_sum(left, right, w_query[:, half_cols:]),
    ]
    kv_parts, _ = lax.optimization_barrier((kv_parts, sums))
    query_chunks, rest = [], [bits, bits[::-1]]
    for held, turns in zip(sums, rest):
        held = held.reshape((2,) * len(bits) + (shard_tokens, half_cols))
        keep, taken, left_axes = halved(held, turns[0], bits[::-1])
        for turn_bit in turns[1:]:
            keep, taken, left_axes = halved(both_sum(keep, taken), turn_bit, left_axes)
        query_chunks.append((keep, taken))
    order = list(range(0, tm_count, 2)) + list(range(1, tm_count, 2))
    within = jnp.arange(shard_tokens, dtype=jnp.int32)
    own_place = late_place * shard_tokens + within
    cosine, sine = rotary_tables(own_place, HDIM)
    kv, scale = finish_keys(kv_parts, cosine, sine, key_cols, block * tm_count)
    all_kv = spread(spread_even(kv))
    key_place = jnp.concatenate([(late_place ^ other) * shard_tokens + within for other in order])
    place_in, counts = shard_count(key_place, late_counts, shard_tokens)
    key_real = (place_in * 4 < counts).astype(jnp.int32)
    attended = attend(
        query_chunks, all_kv, scale, cosine, sine, own_place[:, None], key_place[None, :],
        key_real[None, :], key_cols // HDIM,
    )
    return (conf_out, attended)


def solution(mesh):
    placed = (
        P(("tm", "mp"), None),
        P(),
        P(),
        P(),
        P(),
        P(),
        P(),
        P(),
        P(),
        P(),
        P("tm", "mp"),
        P(),
        P("tm", "mp"),
        P("tm", "mp"),
        P("tm", "mp"),
    )
    return jax.shard_map(
        on_device,
        mesh=mesh,
        in_specs=placed,
        out_specs=(P(("tm", "mp"), None), P("tm", "mp")),
        check_vma=False,
    )
```
